32 devices in a mesh: gx: 4 (over x, core), gy: 8 (over z, y).
Axes of the slice: x: 2, y: 2, z: 4, core: 2. Of those that a mesh axis runs over, the one named last changes fastest.
Arguments:
- fields: float32 [4, 64, 128, 128], P(None, 'gx', 'gy'), may hold values from -6 to 6
- lift: float32 [32, 4], replicated, may hold values from -3 to 3
- lift_bias: float32 [32], replicated, may hold values from -3 to 3
- spectral_in: float32 [256, 2, 8, 32, 64], P(('gx', 'gy')), may hold values from -0.03125 to 0.03125
- bypass_in: float32 [64, 32], replicated, may hold values from -1 to 1
- bias_in: float32 [64], replicated, may hold values from -3 to 3
- spectral_out: float32 [256, 2, 8, 64, 32], P(('gx', 'gy')), may hold values from -0.046875 to 0.046875
- bypass_out: float32 [32, 64], replicated, may hold values from -0.75 to 0.75
- bias_out: float32 [32], replicated, may hold values from -3 to 3
- project: float32 [4, 32], replicated, may hold values from -1 to 1
- project_bias: float32 [4], replicated, may hold values from -3 to 3
Outputs:
- result: float32 [4, 64, 128, 128], P(None, 'gx', 'gy')
The draws below stay inside these ranges and needn't reach their ends.
All inputs are finite; a program needn't handle non-finite values.
Results may differ from the reference program's by a relative error of at most 0.000058.
Values sent between devices are 32-bit elements; how exact they have to be, the bound alone decides.
A program may use at most 64 MiB of HBM per device.

```python
import math
import jax
import jax.numpy as jnp
from jax import lax

CIN = 4
C1 = 32
C2 = 64
KX = 16
KY = 16
KZ = 8
NZ = 128
NX = 64
NY = 128


def wave_table(length, count, offset):
    places = jnp.arange(length, dtype=jnp.int32)
    frequency = jnp.arange(count, dtype=jnp.int32) - offset
    turns = places[:, None] * frequency[None, :] % length
    angle = turns.astype(jnp.float32) * (2.0 * math.pi / length)
    return (jnp.cos(angle), jnp.sin(angle), frequency.astype(jnp.float32))


def draw_fields(key, part):
    key_real = jax.random.fold_in(key, 101)
    key_imag = jax.random.fold_in(key, 202)
    key_rough = jax.random.fold_in(key, 303)
    x_cos, x_sin, freq_x = wave_table(NX, 2 * KX, KX)
    y_cos, y_sin, freq_y = wave_table(NY, 2 * KY, KY)
    z_cos, z_sin, freq_z = wave_table(NZ, 2 * KZ, 0)
    ratio = (freq_x[:, None, None] / KX) ** 2 + (freq_y[None, :, None] / KY) ** 2 + (freq_z[None, None, :] / KZ) ** 2
    amplitude = 1.0 / (1.0 + 2.0 * ratio)
    real_coef = jax.random.normal(key_real, (CIN, 2 * KX, 2 * KY, 2 * KZ), jnp.float32) * amplitude[None]
    imag_coef = jax.random.normal(key_imag, (CIN, 2 * KX, 2 * KY, 2 * KZ), jnp.float32) * amplitude[None]
    highest = lax.Precision.HIGHEST
    real_x = jnp.einsum('cijk,xi->cxjk', real_coef, x_cos, precision=highest) - jnp.einsum('cijk,xi->cxjk', imag_coef, x_sin, precision=highest)
    imag_x = jnp.einsum('cijk,xi->cxjk', real_coef, x_sin, precision=highest) + jnp.einsum('cijk,xi->cxjk', imag_coef, x_cos, precision=highest)
    real_y = jnp.einsum('cxjk,yj->cxyk', real_x, y_cos, precision=highest) - jnp.einsum('cxjk,yj->cxyk', imag_x, y_sin, precision=highest)
    imag_y = jnp.einsum('cxjk,yj->cxyk', real_x, y_sin, precision=highest) + jnp.einsum('cxjk,yj->cxyk', imag_x, y_cos, precision=highest)
    smooth = jnp.einsum('cxyk,zk->cxyz', real_y, z_cos, precision=highest) - jnp.einsum('cxyk,zk->cxyz', imag_y, z_sin, precision=highest)
    smooth = smooth / jnp.sqrt(jnp.sum(amplitude * amplitude))
    rough = jax.random.normal(key_rough, (CIN, NX, NY, NZ), jnp.float32)
    value = smooth + 0.5 * rough
    return jnp.clip(value, -6.0, 6.0)


def levels(rng, dims, pieces, least, top_value):
    level = 1.0
    for position, blocks in pieces:
        draws = jax.random.uniform(jax.random.fold_in(jax.random.fold_in(rng, 6), position), (blocks,), jnp.float32, least / len(pieces), top_value / len(pieces))
        level = level * jnp.repeat(jnp.exp(draws), dims[position] // blocks).reshape((-1,) + (1,) * (len(dims) - 1 - position))
    return level


def gaussian(own_key, extent, deviation, limit, split=(), held_as=jnp.bfloat16):
    values = jax.random.normal(own_key, extent, jnp.float32) * deviation
    if len(split) > 0:
        values = levels(own_key, extent, split, -0.22, 0.18) * values
    return jnp.clip(values, min=-limit, max=limit).astype(held_as)


def setup_inputs(seed: int = 0) -> dict:
    seeds = jax.random.split(jax.random.key(seed), 12)
    return {
        "fields": draw_fields(jax.random.fold_in(seeds[11], 71), 0),
        "lift": gaussian(seeds[1], (C1, CIN), CIN ** -0.5, 3.0, (), jnp.float32),
        "lift_bias": gaussian(seeds[2], (C1,), 0.5, 3.0, (), jnp.float32),
        "spectral_in": gaussian(seeds[3], (KX * KY, 2, KZ, C1, C2), (2 * C1 * NX * NY * NZ // (KX * KY * KZ)) ** -0.5, 0.03125, ((0, 32),), jnp.float32),
        "bypass_in": gaussian(seeds[4], (C2, C1), C1 ** -0.5, 1.0, (), jnp.float32),
        "bias_in": gaussian(seeds[5], (C2,), 0.5, 3.0, (), jnp.float32),
        "spectral_out": gaussian(seeds[6], (KX * KY, 2, KZ, C2, C1), (2 * C2 * NX * NY * NZ // (4 * KX * KY * KZ)) ** -0.5, 0.046875, ((0, 32),), jnp.float32),
        "bypass_out": gaussian(seeds[7], (C1, C2), C2 ** -0.5, 0.75, (), jnp.float32),
        "bias_out": gaussian(seeds[8], (C1,), 0.5, 3.0, (), jnp.float32),
        "project": gaussian(seeds[9], (CIN, C1), C1 ** -0.5, 1.0, (), jnp.float32),
        "project_bias": gaussian(seeds[10], (CIN,), 0.5, 3.0, (), jnp.float32),
    }


def product(formula, left, right):
    return jnp.einsum(formula, left, right, precision=lax.Precision.HIGHEST)

def tables(places, length, count, centered):
    frequency = jnp.arange(count, dtype=jnp.int32)
    if centered:
        frequency = jnp.where(frequency < count // 2, frequency, frequency - count)
    turns = places.astype(jnp.int32)[:, None] * frequency[None, :] % length
    angle = turns.astype(jnp.float32) * (2.0 * math.pi / length)
    return (jnp.cos(angle), jnp.sin(angle))

def forward(field, x_places, y_places, x_length, y_length, scale):
    z_length = field.shape[3]
    z_cos, z_sin = tables(jnp.arange(z_length, dtype=jnp.int32), z_length, KZ, False)
    real_part = product('cxyz,zk->cxyk', field, z_cos)
    imag_part = -product('cxyz,zk->cxyk', field, z_sin)
    y_cos, y_sin = tables(y_places, y_length, KY, True)
    real_next = product('cxyk,yj->cxjk', real_part, y_cos) + product('cxyk,yj->cxjk', imag_part, y_sin)
    imag_next = product('cxyk,yj->cxjk', imag_part, y_cos) - product('cxyk,yj->cxjk', real_part, y_sin)
    x_cos, x_sin = tables(x_places, x_length, KX, True)
    real_last = product('cxjk,xi->ijkc', real_next, x_cos) + product('cxjk,xi->ijkc', imag_next, x_sin)
    imag_last = product('cxjk,xi->ijkc', imag_next, x_cos) - product('cxjk,xi->ijkc', real_next, x_sin)
    stacked = jnp.stack([real_last, imag_last], axis=2)
    return stacked.reshape((KX * KY, 2, KZ, stacked.shape[4])) * scale

def mix_modes(spectrum, weights):
    real_in = spectrum[:, 0]
    imag_in = spectrum[:, 1]
    real_weight = weights[:, 0]
    imag_weight = weights[:, 1]
    real_out = product('mkc,mkcd->mkd', real_in, real_weight) - product('mkc,mkcd->mkd', imag_in, imag_weight)
    imag_out = product('mkc,mkcd->mkd', real_in, imag_weight) + product('mkc,mkcd->mkd', imag_in, real_weight)
    return jnp.stack([real_out, imag_out], axis=1)

def inverse(spectrum, x_places, y_places, x_length, y_length, z_length, scale):
    grid = spectrum.reshape((KX, KY, 2, KZ, spectrum.shape[3]))
    real_part = grid[:, :, 0]
    imag_part = grid[:, :, 1]
    x_cos, x_sin = tables(x_places, x_length, KX, True)
    real_next = product('ijkc,xi->xjkc', real_part, x_cos) - product('ijkc,xi->xjkc', imag_part, x_sin)
    imag_next = product('ijkc,xi->xjkc', real_part, x_sin) + product('ijkc,xi->xjkc', imag_part, x_cos)
    y_cos, y_sin = tables(y_places, y_length, KY, True)
    real_last = product('xjkc,yj->xykc', real_next, y_cos) - product('xjkc,yj->xykc', imag_next, y_sin)
    imag_last = product('xjkc,yj->xykc', real_next, y_sin) + product('xjkc,yj->xykc', imag_next, y_cos)
    z_cos, z_sin = tables(jnp.arange(z_length, dtype=jnp.int32), z_length, KZ, False)
    return (product('xykc,zk->cxyz', real_last, z_cos) - product('xykc,zk->cxyz', imag_last, z_sin)) * scale

def reference(fields, lift, lift_bias, spectral_in, bypass_in, bias_in, spectral_out, bypass_out, bias_out, project, project_bias):
    back = math.sqrt(2.0 / (KX * KY * KZ))
    lifted = product('dc,cxyz->dxyz', lift, fields) + lift_bias[:, None, None, None]
    full_x = jnp.arange(NX, dtype=jnp.int32)
    full_y = jnp.arange(NY, dtype=jnp.int32)
    half_x = jnp.arange(NX // 2, dtype=jnp.int32)
    half_y = jnp.arange(NY // 2, dtype=jnp.int32)
    spectrum = forward(lifted, full_x, full_y, NX, NY, 1.0 / math.sqrt(NX * NY * NZ))
    mixed = mix_modes(spectrum, spectral_in)
    pooled = lifted.reshape((C1, NX // 2, 2, NY // 2, 2, NZ)).mean(axis=(2, 4))
    coarse = jax.nn.gelu(inverse(mixed, 2 * half_x, 2 * half_y, NX, NY, NZ, back) + product('ec,cxyz->exyz', bypass_in, pooled) + bias_in[:, None, None, None], approximate=False)
    spectrum = forward(coarse, half_x, half_y, NX // 2, NY // 2, 1.0 / math.sqrt(NX * NY * NZ / 4.0))
    mixed = mix_modes(spectrum, spectral_out)
    narrow = product('dc,cxyz->dxyz', bypass_out, coarse)
    widened = jnp.repeat(jnp.repeat(narrow, 2, axis=1), 2, axis=2)
    fine = jax.nn.gelu(inverse(mixed, full_x, full_y, NX, NY, NZ, back) + widened + bias_out[:, None, None, None], approximate=False)
    return product('oc,cxyz->oxyz', project, fine + lifted) + project_bias[:, None, None, None]
```

```python
import functools
import math

import jax
import jax.numpy as jnp
import numpy as np
from jax import lax
from jax.experimental import pallas as pl
from jax.experimental.pallas import tpu as pltpu
from jax.sharding import PartitionSpec as P

KX = 16
KY = 16
KZ = 8
YB = 8
LB = 128
F32 = jnp.float32
BF16 = jnp.bfloat16
MESH = pl.DeviceIdType.MESH


def freq(count):
    f = np.arange(count)
    return np.where(f < count // 2, f, f - count)


def halves(table):
    high = table.astype(np.float32).astype(jnp.bfloat16)
    low = (table - high.astype(np.float64)).astype(np.float32).astype(jnp.bfloat16)
    return np.stack([high, low])


def angles(places, frequency, length):
    turns = np.mod(places[:, None] * frequency[None, :], length)
    return turns * (2.0 * math.pi / length)


def z_table(z_length):
    ang = angles(np.arange(z_length), np.arange(KZ), z_length)
    table = np.zeros((YB, z_length, 2, YB, KZ))
    for y in range(YB):
        table[y, :, 0, y] = np.cos(ang)
        table[y, :, 1, y] = -np.sin(ang)
    return table.reshape(YB * z_length, LB)


def y_table(blocks, cells, length, groups):
    per = KY // groups
    frequency = freq(KY)
    out = np.zeros((blocks, cells // YB, 2, YB, KZ, groups, LB))
    for b in range(blocks):
        ang = angles(b * cells + np.arange(cells), frequency, length)
        for y in range(cells):
            for j in range(KY):
                c, s = np.cos(ang[y, j]), np.sin(ang[y, j])
                for k in range(KZ):
                    re = (j % per) * KZ + k
                    im = per * KZ + re
                    at = (b, y // YB)
                    out[at + (0, y % YB, k, j // per, re)] = c
                    out[at + (1, y % YB, k, j // per, re)] = s
                    out[at + (0, y % YB, k, j // per, im)] = -s
                    out[at + (1, y % YB, k, j // per, im)] = c
    return out.reshape(blocks, cells // YB * LB, groups * LB)


def x_angles(blocks, cells, length):
    return angles(np.arange(blocks * cells), freq(KX), length).reshape(blocks, cells, KX)


def split(value):
    high = value.astype(BF16)
    return high, (value - high.astype(F32)).astype(BF16)


def mul(a, b):
    return jnp.dot(a, b, preferred_element_type=F32)


def mul3(a, b):
    return mul(a[0], b[0]) + (mul(a[1], b[0]) + mul(a[0], b[1]))


def gelu(v):
    return (0.5 * v) * (1.0 + lax.erf(v * math.sqrt(0.5)))


def kernel(
    A, B, cells_x, scale1, scale2, gain,
    f_ref, pk_ref, fk_ref, lift_ref, lbias_ref, bp_ref, wo_ref, bo_ref, pr_ref, pl_ref,
    tzf_ref, tzi_ref, cs_ref, w1_hbm, w2_hbm, tx_hbm, yf1_hbm, yfc_hbm, yic_hbm, yi2_hbm,
    o_ref,
    w1, w2, tx, yf1, yfc, yic, yi2,
    buf1, r1, mx, mt1, ag1, yb1, ya1, zc, fx2, r2, buf2, r3, mt2, ag2, yb2, ya2, nar, yr1, yr2,
    csem, ssem, rsem,
):
    a = lax.axis_index("gx")
    b = lax.axis_index("gy")
    me = a * B + b
    IL = KX // A
    H = B // IL
    J = KY // H
    N = A * B
    C1 = lift_ref.shape[0]
    C2 = wo_ref.shape[2]
    CIN = lift_ref.shape[1]
    hx = cells_x // 2

    loads = [
        pltpu.make_async_copy(tx_hbm.at[a], tx, csem.at[0]),
        pltpu.make_async_copy(yf1_hbm.at[b], yf1, csem.at[1]),
        pltpu.make_async_copy(w1_hbm, w1, csem.at[2]),
        pltpu.make_async_copy(yic_hbm.at[b], yic, csem.at[3]),
        pltpu.make_async_copy(yfc_hbm.at[b], yfc, csem.at[4]),
        pltpu.make_async_copy(w2_hbm, w2, csem.at[5]),
        pltpu.make_async_copy(yi2_hbm.at[b], yi2, csem.at[6]),
    ]
    for load in loads:
        load.start()

    barrier = pltpu.get_barrier_semaphore()
    for step in range(1, N):
        peer = lax.rem(me + step, N)
        pl.semaphore_signal(
            barrier, inc=1, device_id=(peer // B, lax.rem(peer, B)), device_id_type=MESH
        )

    lane = lax.broadcasted_iota(jnp.int32, (1, LB), 1)
    sign_f = jnp.where(lane < LB // 2, 1.0, -1.0).astype(F32)

    def rot_f(v):
        return pltpu.roll(v, LB // 2, 1) * sign_f

    def rot_i(v):
        return pltpu.roll(v, LB // 2, 1) * -sign_f

    tzf = (tzf_ref[0], tzf_ref[1])
    width = tzf_ref.shape[1]
    zs = []
    for ch in range(2):
        zs.append(mul3(split(f_ref[:, ch * width:(ch + 1) * width]), tzf))
    loads[0].wait()
    us = []
    for z in zs:
        us.append(mul3((tx[0], tx[1]), split(jnp.concatenate([z, rot_f(z)], axis=0))))
    loads[1].wait()
    part = mul3(split(jnp.concatenate(us, axis=1)), (yf1[0], yf1[1]))
    for i in range(KX):
        for h in range(H):
            buf1[i * H + h] = part[i * CIN:(i + 1) * CIN, h * LB:(h + 1) * LB]
    r1[me] = buf1[me]
    pl.semaphore_wait(barrier, N - 1)

    sends = []
    phase = []
    for step in range(1, N):
        peer = lax.rem(me + step, N)
        phase.append(pltpu.make_async_remote_copy(
            src_ref=buf1.at[peer], dst_ref=r1.at[me], send_sem=ssem.at[peer], recv_sem=rsem.at[me],
            device_id=(peer // B, lax.rem(peer, B)), device_id_type=MESH,
        ))
    for copy in phase:
        copy.start()
    sends += phase
    loads[2].wait()
    for step in range(1, N):
        peer = lax.rem(me + step, N)
        pltpu.make_async_remote_copy(
            src_ref=buf1.at[peer], dst_ref=r1.at[peer], send_sem=ssem.at[peer], recv_sem=rsem.at[peer],
            device_id=(peer // B, lax.rem(peer, B)), device_id_type=MESH,
        ).wait_recv()

    first_slot = {1: N, 2: N + B, 3: N + B + A, 4: N + B + 2 * A, 5: N + 2 * B + 2 * A, 6: N + 3 * B + 2 * A}

    def spread(source, target, axis, count, mine, slot):
        copies = []
        arrivals = []
        base = first_slot[slot]
        for step in range(1, count):
            peer = lax.rem(mine + step, count)
            where = (peer, b) if axis == "gx" else (a, peer)
            for index, group in ((mine, copies), (peer, arrivals)):
                group.append(pltpu.make_async_remote_copy(
                    src_ref=source(peer), dst_ref=target.at[index],
                    send_sem=ssem.at[base + peer], recv_sem=rsem.at[base + index],
                    device_id=where, device_id_type=MESH,
                ))
        for copy in copies:
            copy.start()
        sends.extend(copies)
        return arrivals

    def arrive(copies):
        for copy in copies:
            copy.wait_recv()

    def mix(st, w, width_out):
        mx[...] = jnp.zeros_like(mx)
        for j in range(J):
            for k in range(KZ):
                q = j * KZ + k
                p = J * KZ + q
                re = st[:, q:q + 1]
                im = st[:, p:p + 1]
                wr = w[j, 0, k]
                wi = w[j, 1, k]
                mx[q:q + 1, :width_out] = jnp.sum(re * wr - im * wi, axis=0, keepdims=True)
                mx[p:p + 1, :width_out] = jnp.sum(re * wi + im * wr, axis=0, keepdims=True)
        return mx[...].T[:width_out]

    s4 = jnp.sum(r1[...], axis=0) * scale1
    st = lift_ref[:, 0:1] * s4[0:1]
    for c in range(1, CIN):
        st = st + lift_ref[:, c:c + 1] * s4[c:c + 1]
    first = jnp.where((lane == 0) & (me == 0), gain, 0.0).astype(F32)
    st = st + lbias_ref[...] * first
    mixed = mix(st, w1, C2)
    mt1[...] = mixed
    ag1[b] = mixed
    copies = spread(lambda peer: mt1, ag1, "gy", B, b, 1)
    loads[3].wait()
    arrive(copies)

    def y_back(ag, table):
        rows = [jnp.concatenate([ag[i * H + h] for i in range(IL)], axis=0) for h in range(H)]
        return mul3(split(jnp.concatenate(rows, axis=1)), (table[0], table[1]))

    y = y_back(ag1, yic).reshape(IL, C2, LB)
    yb1[...] = y
    ya1[a] = y
    arrive(spread(lambda peer: yb1, ya1, "gx", A, a, 2))
    for i in range(KX):
        yr1[i] = rot_i(ya1[i // IL, i % IL])

    HC = hx * KX

    def coarse_step(x, carry):
        acc = jnp.zeros((C2, LB), F32)
        for i in range(KX):
            c = cs_ref[a, x * KX + i]
            s = cs_ref[a, HC + x * KX + i]
            acc = acc + (c * ya1[i // IL, i % IL] + s * yr1[i])
        v = mul3(split(acc), (tzi_ref[0], tzi_ref[1])) + mul(bp_ref[...], pk_ref[x])
        g = split(gelu(v))
        nar[x] = mul3((wo_ref[0], wo_ref[1]), g)
        zc[x] = mul3(g, (tzf_ref[0], tzf_ref[1]))
        return carry

    lax.fori_loop(0, hx, coarse_step, 0)

    def x_step(i, carry):
        re = jnp.zeros((C2, LB), F32)
        im = jnp.zeros((C2, LB), F32)
        for x in range(hx):
            re = re + cs_ref[a, x * KX + i] * zc[x]
            im = im + cs_ref[a, HC + x * KX + i] * zc[x]
        fx2[i // IL, i % IL] = re + rot_f(im)
        return carry

    lax.fori_loop(0, KX, x_step, 0)
    copies = spread(lambda peer: fx2.at[peer], r2, "gx", A, a, 3)
    r2[a] = fx2[a]
    loads[4].wait()
    arrive(copies)
    total = jnp.sum(r2[...], axis=0).reshape(IL * C2, LB)
    out = mul3(split(total), (yfc[0], yfc[1]))
    for i in range(IL):
        for h in range(H):
            buf2[i * H + h] = out[i * C2:(i + 1) * C2, h * LB:(h + 1) * LB]
    copies = spread(lambda peer: buf2.at[peer], r3, "gy", B, b, 4)
    r3[b] = buf2[b]
    loads[5].wait()
    arrive(copies)
    st = jnp.sum(r3[...], axis=0) * scale2
    mixed = mix(st, w2, C1)
    mt2[...] = mixed
    ag2[b] = mixed
    copies = spread(lambda peer: mt2, ag2, "gy", B, b, 5)
    loads[6].wait()
    arrive(copies)
    y = y_back(ag2, yi2).reshape(IL, C1, 2 * LB)
    yb2[...] = y
    ya2[a] = y
    arrive(spread(lambda peer: yb2, ya2, "gx", A, a, 6))
    for i in range(KX):
        for ch in range(2):
            part = slice(ch * LB, (ch + 1) * LB)
            yr2[i, :, part] = rot_i(ya2[i // IL, i % IL, :, part])

    FC = cells_x * KX
    zn = width // YB

    def fine_step(x, carry):
        acc = jnp.zeros((C1, 2 * LB), F32)
        for i in range(KX):
            c = cs_ref[a, 2 * HC + x * KX + i]
            s = cs_ref[a, 2 * HC + FC + x * KX + i]
            acc = acc + (c * ya2[i // IL, i % IL] + s * yr2[i])
        for ch in range(2):
            v = mul3(split(acc[:, ch * LB:(ch + 1) * LB]), (tzi_ref[0], tzi_ref[1]))
            pieces = []
            for yy in range(YB):
                at = (ch * YB + yy) // 2 * zn
                pieces.append(nar[x // 2, :, at:at + zn])
            v = v + jnp.concatenate(pieces, axis=1) + bo_ref[...]
            g = split(gelu(v))
            cols = slice(ch * width, (ch + 1) * width)
            o_ref[x, :, cols] = mul3((pr_ref[0], pr_ref[1]), g) + mul(pl_ref[...], fk_ref[x, :, cols])
        return carry

    lax.fori_loop(0, cells_x, fine_step, 0)
    for copy in sends:
        copy.wait_send()


def rough(value):
    return lax.reduce_precision(value, 8, 7)


def hi_lo(value):
    high = rough(value)
    return jnp.stack([high.astype(BF16), rough(value - high).astype(BF16)])


def left16(matrix, bias):
    high = rough(matrix)
    low = rough(matrix - high)
    b0 = rough(bias)
    b1 = rough(bias - b0)
    b2 = rough(bias - b0 - b1)
    zero = jnp.zeros((matrix.shape[0], 1), F32)
    return jnp.concatenate(
        [high, high, low, b0[:, None], b1[:, None], b2[:, None], zero], axis=1
    ).astype(BF16)


def right16(value):
    high = rough(value)
    low = rough(value - high)
    ones = jnp.ones((value.shape[0], 4, value.shape[2]), F32)
    return jnp.concatenate([high, low, high, ones], axis=1).astype(BF16)


def product(left, right):
    return jnp.dot(left, right, precision=lax.Precision.HIGHEST)


def on_device(
    A, B, fields, lift, lift_bias, spectral_in, bypass_in, bias_in, spectral_out, bypass_out,
    bias_out, proj, proj_bias,
):
    cin, xc, yc, zc = fields.shape
    C1 = lift.shape[0]
    C2 = bypass_in.shape[0]
    NX = xc * A
    NY = yc * B
    IL = KX // A
    H = B // IL
    J = KY // H
    N = A * B
    width = YB * zc
    cells = float(NX * NY * zc)
    back = math.sqrt(2.0 / (KX * KY * KZ))

    tz = z_table(zc)
    tzf = halves(tz)
    tzi = halves(np.ascontiguousarray(tz.T) * back)
    fine_x = x_angles(A, xc, NX)
    half_x = x_angles(A, xc // 2, NX // 2)
    eye = np.eye(cin)
    tx = np.stack([
        np.concatenate([np.kron(np.cos(fine_x[i].T), eye), np.kron(np.sin(fine_x[i].T), eye)], axis=1)
        for i in range(A)
    ])
    cs = np.concatenate([
        np.cos(half_x).reshape(A, -1), np.sin(half_x).reshape(A, -1),
        np.cos(fine_x).reshape(A, -1), np.sin(fine_x).reshape(A, -1),
    ], axis=1).astype(np.float32)
    yf1 = y_table(B, yc, NY, H)
    yfc = y_table(B, yc // 2, NY // 2, H)

    def per_device(table):
        return jnp.asarray(np.ascontiguousarray(np.swapaxes(halves(table), 0, 1)))

    tx_t = per_device(tx)
    yf1_t = per_device(yf1)
    yfc_t = per_device(yfc)
    yic_t = per_device(np.swapaxes(yfc, 1, 2))
    yi2_t = per_device(np.swapaxes(yf1, 1, 2))

    rows = jnp.transpose(fields, (1, 0, 2, 3)).reshape(xc, cin, yc * zc)
    pooled = fields.reshape(cin, xc // 2, 2, yc // 2, 2, zc).mean(axis=(2, 4))
    pooled = jnp.transpose(pooled, (1, 0, 2, 3)).reshape(xc // 2, cin, width)
    bp = left16(product(bypass_in, lift), product(bypass_in, lift_bias) + bias_in)
    pj = left16(product(proj, lift), product(proj, lift_bias) + proj_bias)

    vmem = pl.BlockSpec(memory_space=pltpu.VMEM)
    anywhere = pl.BlockSpec(memory_space=pl.ANY)
    V = pltpu.VMEM
    out = pl.pallas_call(
        functools.partial(
            kernel, A, B, xc, 1.0 / math.sqrt(cells), 1.0 / math.sqrt(cells / 4.0), math.sqrt(cells)
        ),
        out_shape=jax.ShapeDtypeStruct((xc, cin, yc * zc), F32),
        in_specs=[vmem] * 12 + [pl.BlockSpec(memory_space=pltpu.SMEM)] + [anywhere] * 7,
        out_specs=vmem,
        scratch_shapes=[
            V(spectral_in.shape, F32), V(spectral_out.shape, F32),
            V(tx_t.shape[1:], BF16), V(yf1_t.shape[1:], BF16), V(yfc_t.shape[1:], BF16),
            V(yic_t.shape[1:], BF16), V(yi2_t.shape[1:], BF16),
            V((N, cin, LB), F32), V((N, cin, LB), F32), V((LB, LB), F32),
            V((C2, LB), F32), V((B, C2, LB), F32),
            V((IL, C2, LB), F32), V((A, IL, C2, LB), F32),
            V((xc // 2, C2, LB), F32), V((A, IL, C2, LB), F32), V((A, IL, C2, LB), F32),
            V((B, C2, LB), F32), V((B, C2, LB), F32),
            V((C1, LB), F32), V((B, C1, LB), F32),
            V((IL, C1, 2 * LB), F32), V((A, IL, C1, 2 * LB), F32),
            V((xc // 2, C1, width), F32), V((KX, C2, LB), F32), V((KX, C1, 2 * LB), F32),
            pltpu.SemaphoreType.DMA((7,)),
            pltpu.SemaphoreType.DMA((N + 3 * B + 3 * A,)), pltpu.SemaphoreType.DMA((N + 3 * B + 3 * A,)),
        ],
        compiler_params=pltpu.CompilerParams(
            collective_id=0, has_side_effects=True, vmem_limit_bytes=60 * 1024 * 1024
        ),
    )(
        rows.reshape(xc * cin, yc * zc), right16(pooled), right16(rows), lift, lift_bias[:, None], bp,
        hi_lo(bypass_out), bias_out[:, None], hi_lo(proj), pj, jnp.asarray(tzf), jnp.asarray(tzi),
        jnp.asarray(cs), spectral_in, spectral_out, tx_t, yf1_t, yfc_t, yic_t, yi2_t,
    )
    return jnp.transpose(out.reshape(xc, cin, yc, zc), (1, 0, 2, 3))


def solution(mesh):
    A = mesh.shape["gx"]
    B = mesh.shape["gy"]
    in_specs = (
        P(None, "gx", "gy", None), P(), P(), P(("gx", "gy"), None, None, None, None), P(), P(),
        P(("gx", "gy"), None, None, None, None), P(), P(), P(), P(),
    )
    return jax.shard_map(
        functools.partial(on_device, A, B), mesh=mesh, in_specs=in_specs,
        out_specs=P(None, "gx", "gy", None), check_vma=False,
    )
```

```python
import functools
import math

import jax
import jax.numpy as jnp
import numpy as np
from jax import lax
from jax.experimental import pallas as pl
from jax.experimental.pallas import tpu as pltpu
from jax.sharding import PartitionSpec as P

KX = 16
KY = 16
KZ = 8
YB = 8
LB = 128
F32 = jnp.float32
BF16 = jnp.bfloat16
MESH = pl.DeviceIdType.MESH


def freq(count):
    f = np.arange(count)
    return np.where(f < count // 2, f, f - count)


def halves(table):
    high = table.astype(np.float32).astype(jnp.bfloat16)
    low = (table - high.astype(np.float64)).astype(np.float32).astype(jnp.bfloat16)
    return np.stack([high, low])


def angles(places, frequency, length):
    turns = np.mod(places[:, None] * frequency[None, :], length)
    return turns * (2.0 * math.pi / length)


def z_table(z_length):
    ang = angles(np.arange(z_length), np.arange(KZ), z_length)
    table = np.zeros((YB, z_length, 2, YB, KZ))
    for y in range(YB):
        table[y, :, 0, y] = np.cos(ang)
        table[y, :, 1, y] = -np.sin(ang)
    return table.reshape(YB * z_length, LB)


def y_table(blocks, cells, length, groups):
    per = KY // groups
    frequency = freq(KY)
    out = np.zeros((blocks, cells // YB, 2, YB, KZ, groups, LB))
    for b in range(blocks):
        ang = angles(b * cells + np.arange(cells), frequency, length)
        for y in range(cells):
            for j in range(KY):
                c, s = np.cos(ang[y, j]), np.sin(ang[y, j])
                for k in range(KZ):
                    re = (j % per) * KZ + k
                    im = per * KZ + re
                    at = (b, y // YB)
                    out[at + (0, y % YB, k, j // per, re)] = c
                    out[at + (1, y % YB, k, j // per, re)] = s
                    out[at + (0, y % YB, k, j // per, im)] = -s
                    out[at + (1, y % YB, k, j // per, im)] = c
    return out.reshape(blocks, cells // YB * LB, groups * LB)


def x_angles(blocks, cells, length):
    return angles(np.arange(blocks * cells), freq(KX), length).reshape(blocks, cells, KX)


def split(value):
    high = value.astype(BF16)
    return high, (value - high.astype(F32)).astype(BF16)


def mul(a, b):
    return jnp.dot(a, b, preferred_element_type=F32)


def mul3(a, b):
    return mul(a[0], b[0]) + (mul(a[1], b[0]) + mul(a[0], b[1]))


def gelu(v):
    return (0.5 * v) * (1.0 + lax.erf(v * math.sqrt(0.5)))


def kernel(
    A, B, cells_x, scale1, scale2, gain,
    f_ref, lift_ref, lbias_ref, byp_ref, bi_ref, wo_ref, bo_ref, pr_ref, pb_ref,
    tzf_ref, tzi_ref, cs_ref, w1_hbm, w2_hbm, tx_hbm, yf1_hbm, yfc_hbm, yic_hbm, yi2_hbm,
    o_ref,
    w1, w2, tx, yf1, yfc, yic, yi2,
    buf1, r1, mx, mt1, ag1, yb1, ya1, zc, fx2, r2, buf2, r3, mt2, ag2, yb2, ya2, nar, yr1, yr2, pk_ref, fk_ref, t16,
    csem, ssem, rsem,
):
    a = lax.axis_index("gx")
    b = lax.axis_index("gy")
    me = a * B + b
    IL = KX // A
    H = B // IL
    J = KY // H
    N = A * B
    CIN, C1 = lift_ref.shape
    C2 = wo_ref.shape[1]
    hx = cells_x // 2

    loads = [
        pltpu.make_async_copy(tx_hbm.at[a], tx, csem.at[0]),
        pltpu.make_async_copy(yf1_hbm.at[b], yf1, csem.at[1]),
        pltpu.make_async_copy(w1_hbm, w1, csem.at[2]),
        pltpu.make_async_copy(yic_hbm.at[b], yic, csem.at[3]),
        pltpu.make_async_copy(yfc_hbm.at[b], yfc, csem.at[4]),
        pltpu.make_async_copy(w2_hbm, w2, csem.at[5]),
        pltpu.make_async_copy(yi2_hbm.at[b], yi2, csem.at[6]),
    ]
    for load in loads:
        load.start()

    barrier = pltpu.get_barrier_semaphore()
    for step in range(1, N):
        peer = lax.rem(me + step, N)
        pl.semaphore_signal(
            barrier, inc=1, device_id=(peer // B, lax.rem(peer, B)), device_id_type=MESH
        )

    lane = lax.broadcasted_iota(jnp.int32, (1, LB), 1)
    sign_f = jnp.where(lane < LB // 2, 1.0, -1.0).astype(F32)

    def rot_f(v):
        return pltpu.roll(v, LB // 2, 1) * sign_f

    def rot_i(v):
        return pltpu.roll(v, LB // 2, 1) * -sign_f

    tzf = (tzf_ref[0], tzf_ref[1])
    width = tzf_ref.shape[1]
    zs = []
    for ch in range(2):
        zs.append(mul3(split(f_ref[:, ch * width:(ch + 1) * width]), tzf))
    loads[0].wait()
    us = []
    for z in zs:
        us.append(mul3((tx[0], tx[1]), split(jnp.concatenate([z, rot_f(z)], axis=0))))
    loads[1].wait()
    part = mul3(split(jnp.concatenate(us, axis=1)), (yf1[0], yf1[1]))
    for i in range(KX):
        for h in range(H):
            buf1[i * H + h] = part[i * CIN:(i + 1) * CIN, h * LB:(h + 1) * LB]
    r1[me] = buf1[me]
    pl.semaphore_wait(barrier, N - 1)

    sends = []
    phase = []
    for step in range(1, N):
        peer = lax.rem(me + step, N)
        phase.append(pltpu.make_async_remote_copy(
            src_ref=buf1.at[peer], dst_ref=r1.at[me], send_sem=ssem.at[peer], recv_sem=rsem.at[me],
            device_id=(peer // B, lax.rem(peer, B)), device_id_type=MESH,
        ))
    for copy in phase:
        copy.start()
    sends += phase
    loads[2].wait()
    mx[...] = jnp.zeros_like(mx)
    mx[0:CIN, :C1] = lift_ref[...]
    mx[CIN:CIN + 1, :C1] = lbias_ref[...]
    mx[CIN + 1:CIN + 2, :C1] = bo_ref[...]
    lift8 = jnp.concatenate([mx[0:8, :C1]], axis=0)
    columns = mx[...].T[:C1]
    bo_col = columns[:, CIN + 1:CIN + 2]

    def left16(matrix, bias):
        n = matrix.shape[1]
        high, low = split(matrix[0:CIN])
        b0 = bias.astype(BF16)
        rest = bias - b0.astype(F32)
        b1 = rest.astype(BF16)
        b2 = (rest - b1.astype(F32)).astype(BF16)
        mx[...] = jnp.zeros_like(mx)
        mx[0:CIN, :n] = high.astype(F32)
        mx[CIN:2 * CIN, :n] = high.astype(F32)
        mx[2 * CIN:3 * CIN, :n] = low.astype(F32)
        for row, value in enumerate((b0, b1, b2)):
            mx[3 * CIN + row:3 * CIN + row + 1, :n] = value.astype(F32)
        return mx[...].T[:n, :16].astype(BF16)

    highest = lax.Precision.HIGHEST
    m = jnp.dot(lift8, byp_ref[...], precision=highest, preferred_element_type=F32)
    bp16 = left16(m, m[CIN:CIN + 1] + bi_ref[...])
    m = lax.dot_general(
        lift8, pr_ref[...], (((1,), (1,)), ((), ())), precision=highest, preferred_element_type=F32
    )
    pl16 = left16(m, m[CIN:CIN + 1] + pb_ref[...])
    wo2 = split(wo_ref[...])
    pr2 = split(pr_ref[...])
    t16[...] = jnp.ones_like(t16)
    for step in range(1, N):
        peer = lax.rem(me + step, N)
        pltpu.make_async_remote_copy(
            src_ref=buf1.at[peer], dst_ref=r1.at[peer], send_sem=ssem.at[peer], recv_sem=rsem.at[peer],
            device_id=(peer // B, lax.rem(peer, B)), device_id_type=MESH,
        ).wait_recv()

    first_slot = {1: N, 2: N + B, 3: N + B + A, 4: N + B + 2 * A, 5: N + 2 * B + 2 * A, 6: N + 3 * B + 2 * A}

    def spread(source, target, axis, count, mine, slot):
        copies = []
        arrivals = []
        base = first_slot[slot]
        for step in range(1, count):
            peer = lax.rem(mine + step, count)
            where = (peer, b) if axis == "gx" else (a, peer)
            for index, group in ((mine, copies), (peer, arrivals)):
                group.append(pltpu.make_async_remote_copy(
                    src_ref=source(peer), dst_ref=target.at[index],
                    send_sem=ssem.at[base + peer], recv_sem=rsem.at[base + index],
                    device_id=where, device_id_type=MESH,
                ))
        for copy in copies:
            copy.start()
        sends.extend(copies)
        return arrivals

    def arrive(copies):
        for copy in copies:
            copy.wait_recv()

    def mix(st, w, width_out):
        mx[...] = jnp.zeros_like(mx)
        for j in range(J):
            for k in range(KZ):
                q = j * KZ + k
                p = J * KZ + q
                re = st[:, q:q + 1]
                im = st[:, p:p + 1]
                wr = w[j, 0, k]
                wi = w[j, 1, k]
                mx[q:q + 1, :width_out] = jnp.sum(re * wr - im * wi, axis=0, keepdims=True)
                mx[p:p + 1, :width_out] = jnp.sum(re * wi + im * wr, axis=0, keepdims=True)
        return mx[...].T[:width_out]

    s4 = jnp.sum(r1[...], axis=0) * scale1
    st = columns[:, 0:1] * s4[0:1]
    for c in range(1, CIN):
        st = st + columns[:, c:c + 1] * s4[c:c + 1]
    first = jnp.where((lane == 0) & (me == 0), gain, 0.0).astype(F32)
    st = st + columns[:, CIN:CIN + 1] * first
    mixed = mix(st, w1, C2)
    mt1[...] = mixed
    ag1[b] = mixed
    copies = spread(lambda peer: mt1, ag1, "gy", B, b, 1)
    zn = width // YB

    def fill(value):
        n = value.shape[1]
        high, low = split(value)
        t16[0:CIN, :n] = high.astype(F32)
        t16[CIN:2 * CIN, :n] = low.astype(F32)
        t16[2 * CIN:3 * CIN, :n] = high.astype(F32)
        return t16[:, :n].astype(BF16)

    for x in range(hx):
        one = f_ref[2 * x * CIN:(2 * x + 1) * CIN]
        two = f_ref[(2 * x + 1) * CIN:(2 * x + 2) * CIN]
        fk_ref[2 * x] = fill(one)
        fk_ref[2 * x + 1] = fill(two)
        both = one + two
        pieces = [
            both[:, 2 * y * zn:(2 * y + 1) * zn] + both[:, (2 * y + 1) * zn:(2 * y + 2) * zn]
            for y in range(YB)
        ]
        pk_ref[x] = fill(jnp.concatenate(pieces, axis=1) * 0.25)
    loads[3].wait()
    arrive(copies)

    def y_back(ag, table):
        rows = [jnp.concatenate([ag[i * H + h] for i in range(IL)], axis=0) for h in range(H)]
        return mul3(split(jnp.concatenate(rows, axis=1)), (table[0], table[1]))

    y = y_back(ag1, yic).reshape(IL, C2, LB)
    yb1[...] = y
    ya1[a] = y
    arrive(spread(lambda peer: yb1, ya1, "gx", A, a, 2))
    for i in range(KX):
        yr1[i] = rot_i(ya1[i // IL, i % IL])

    HC = hx * KX

    def coarse_step(x, carry):
        acc = jnp.zeros((C2, LB), F32)
        for i in range(KX):
            c = cs_ref[a, x * KX + i]
            s = cs_ref[a, HC + x * KX + i]
            acc = acc + (c * ya1[i // IL, i % IL] + s * yr1[i])
        v = mul3(split(acc), (tzi_ref[0], tzi_ref[1])) + mul(bp16, pk_ref[x])
        g = split(gelu(v))
        nar[x] = mul3(wo2, g)
        zc[x] = mul3(g, (tzf_ref[0], tzf_ref[1]))
        return carry

    lax.fori_loop(0, hx, coarse_step, 0)

    def x_step(i, carry):
        re = jnp.zeros((C2, LB), F32)
        im = jnp.zeros((C2, LB), F32)
        for x in range(hx):
            re = re + cs_ref[a, x * KX + i] * zc[x]
            im = im + cs_ref[a, HC + x * KX + i] * zc[x]
        fx2[i // IL, i % IL] = re + rot_f(im)
        return carry

    lax.fori_loop(0, KX, x_step, 0)
    copies = spread(lambda peer: fx2.at[peer], r2, "gx", A, a, 3)
    r2[a] = fx2[a]
    loads[4].wait()
    arrive(copies)
    total = jnp.sum(r2[...], axis=0).reshape(IL * C2, LB)
    out = mul3(split(total), (yfc[0], yfc[1]))
    for i in range(IL):
        for h in range(H):
            buf2[i * H + h] = out[i * C2:(i + 1) * C2, h * LB:(h + 1) * LB]
    copies = spread(lambda peer: buf2.at[peer], r3, "gy", B, b, 4)
    r3[b] = buf2[b]
    loads[5].wait()
    arrive(copies)
    st = (jnp.sum(r3[...], axis=0) * scale2).T
    mixed = jnp.zeros((C1, LB), F32)
    for j in range(J):
        for k in range(KZ):
            q = j * KZ + k
            p = J * KZ + q
            re = st[q:q + 1]
            im = st[p:p + 1]
            wr = w2[j, 0, k]
            wi = w2[j, 1, k]
            real = jnp.sum(re * wr - im * wi, axis=1, keepdims=True)
            imag = jnp.sum(re * wi + im * wr, axis=1, keepdims=True)
            mixed = jnp.where(lane == q, real, jnp.where(lane == p, imag, mixed))
    mt2[...] = mixed
    ag2[b] = mixed
    copies = spread(lambda peer: mt2, ag2, "gy", B, b, 5)
    loads[6].wait()
    arrive(copies)
    y = y_back(ag2, yi2).reshape(IL, C1, 2 * LB)
    yb2[...] = y
    ya2[a] = y
    arrive(spread(lambda peer: yb2, ya2, "gx", A, a, 6))
    for i in range(KX):
        for ch in range(2):
            part = slice(ch * LB, (ch + 1) * LB)
            yr2[i, :, part] = rot_i(ya2[i // IL, i % IL, :, part])

    FC = cells_x * KX

    def fine_step(x, carry):
        acc = jnp.zeros((C1, 2 * LB), F32)
        for i in range(KX):
            c = cs_ref[a, 2 * HC + x * KX + i]
            s = cs_ref[a, 2 * HC + FC + x * KX + i]
            acc = acc + (c * ya2[i // IL, i % IL] + s * yr2[i])
        for ch in range(2):
            v = mul3(split(acc[:, ch * LB:(ch + 1) * LB]), (tzi_ref[0], tzi_ref[1]))
            pieces = []
            for yy in range(YB):
                at = (ch * YB + yy) // 2 * zn
                pieces.append(nar[x // 2, :, at:at + zn])
            v = v + jnp.concatenate(pieces, axis=1) + bo_col
            g = split(gelu(v))
            cols = slice(ch * width, (ch + 1) * width)
            o_ref[x, :, cols] = mul3(pr2, g) + mul(pl16, fk_ref[x, :, cols])
        return carry

    lax.fori_loop(0, cells_x, fine_step, 0)
    for copy in sends:
        copy.wait_send()


def on_device(
    A, B, fields, lift, lift_bias, spectral_in, bypass_in, bias_in, spectral_out, bypass_out,
    bias_out, proj, proj_bias,
):
    cin, xc, yc, zc = fields.shape
    C1 = lift.shape[0]
    C2 = bypass_in.shape[0]
    NX = xc * A
    NY = yc * B
    IL = KX // A
    H = B // IL
    J = KY // H
    N = A * B
    width = YB * zc
    cells = float(NX * NY * zc)
    back = math.sqrt(2.0 / (KX * KY * KZ))

    tz = z_table(zc)
    tzf = halves(tz)
    tzi = halves(np.ascontiguousarray(tz.T) * back)
    fine_x = x_angles(A, xc, NX)
    half_x = x_angles(A, xc // 2, NX // 2)
    eye = np.eye(cin)
    tx = np.stack([
        np.concatenate([np.kron(np.cos(fine_x[i].T), eye), np.kron(np.sin(fine_x[i].T), eye)], axis=1)
        for i in range(A)
    ])
    cs = np.concatenate([
        np.cos(half_x).reshape(A, -1), np.sin(half_x).reshape(A, -1),
        np.cos(fine_x).reshape(A, -1), np.sin(fine_x).reshape(A, -1),
    ], axis=1).astype(np.float32)
    yf1 = y_table(B, yc, NY, H)
    yfc = y_table(B, yc // 2, NY // 2, H)

    def per_device(table):
        return jnp.asarray(np.ascontiguousarray(np.swapaxes(halves(table), 0, 1)))

    tx_t = per_device(tx)
    yf1_t = per_device(yf1)
    yfc_t = per_device(yfc)
    yic_t = per_device(np.swapaxes(yfc, 1, 2))
    yi2_t = per_device(np.swapaxes(yf1, 1, 2))

    rows = jnp.transpose(fields, (1, 0, 2, 3)).reshape(xc * cin, yc * zc)
    weights2 = jnp.swapaxes(spectral_out, 3, 4)

    vmem = pl.BlockSpec(memory_space=pltpu.VMEM)
    anywhere = pl.BlockSpec(memory_space=pl.ANY)
    V = pltpu.VMEM
    out = pl.pallas_call(
        functools.partial(
            kernel, A, B, xc, 1.0 / math.sqrt(cells), 1.0 / math.sqrt(cells / 4.0), math.sqrt(cells)
        ),
        out_shape=jax.ShapeDtypeStruct((xc, cin, yc * zc), F32),
        in_specs=[vmem] * 11 + [pl.BlockSpec(memory_space=pltpu.SMEM)] + [anywhere] * 7,
        out_specs=vmem,
        scratch_shapes=[
            V(spectral_in.shape, F32), V(weights2.shape, F32),
            V(tx_t.shape[1:], BF16), V(yf1_t.shape[1:], BF16), V(yfc_t.shape[1:], BF16),
            V(yic_t.shape[1:], BF16), V(yi2_t.shape[1:], BF16),
            V((N, cin, LB), F32), V((N, cin, LB), F32), V((LB, LB), F32),
            V((C2, LB), F32), V((B, C2, LB), F32),
            V((IL, C2, LB), F32), V((A, IL, C2, LB), F32),
            V((xc // 2, C2, LB), F32), V((A, IL, C2, LB), F32), V((A, IL, C2, LB), F32),
            V((B, C2, LB), F32), V((B, C2, LB), F32),
            V((C1, LB), F32), V((B, C1, LB), F32),
            V((IL, C1, 2 * LB), F32), V((A, IL, C1, 2 * LB), F32),
            V((xc // 2, C1, width), F32), V((KX, C2, LB), F32), V((KX, C1, 2 * LB), F32),
            V((xc // 2, 16, width), BF16), V((xc, 16, yc * zc), BF16), V((16, yc * zc), F32),
            pltpu.SemaphoreType.DMA((7,)),
            pltpu.SemaphoreType.DMA((N + 3 * B + 3 * A,)), pltpu.SemaphoreType.DMA((N + 3 * B + 3 * A,)),
        ],
        compiler_params=pltpu.CompilerParams(
            collective_id=0, has_side_effects=True, vmem_limit_bytes=60 * 1024 * 1024
        ),
    )(
        rows, lift.T, lift_bias[None], bypass_in.T, bias_in[None], bypass_out, bias_out[None], proj,
        proj_bias[None], jnp.asarray(tzf), jnp.asarray(tzi),
        jnp.asarray(cs), spectral_in, weights2, tx_t, yf1_t, yfc_t, yic_t, yi2_t,
    )
    return jnp.transpose(out.reshape(xc, cin, yc, zc), (1, 0, 2, 3))


def solution(mesh):
    A = mesh.shape["gx"]
    B = mesh.shape["gy"]
    in_specs = (
        P(None, "gx", "gy", None), P(), P(), P(("gx", "gy"), None, None, None, None), P(), P(),
        P(("gx", "gy"), None, None, None, None), P(), P(), P(), P(),
    )
    return jax.shard_map(
        functools.partial(on_device, A, B), mesh=mesh, in_specs=in_specs,
        out_specs=P(None, "gx", "gy", None), check_vma=False,
    )
```

```python
import functools
import math

import jax
import jax.numpy as jnp
import numpy as np
from jax import lax
from jax.experimental import pallas as pl
from jax.experimental.pallas import tpu as pltpu
from jax.sharding import PartitionSpec as P

KX = 16
KY = 16
KZ = 8
YB = 8
LB = 128
GROUP = 4
F32 = jnp.float32
BF16 = jnp.bfloat16
MESH = pl.DeviceIdType.MESH


def freq(count):
    f = np.arange(count)
    return np.where(f < count // 2, f, f - count)


def halves(table):
    high = table.astype(np.float32).astype(jnp.bfloat16)
    low = (table - high.astype(np.float64)).astype(np.float32).astype(jnp.bfloat16)
    return np.stack([high, low])


def stacked(table):
    high, low = halves(table)
    return np.concatenate([high, high, low], axis=0)


def angles(places, frequency, length):
    turns = np.mod(places[:, None] * frequency[None, :], length)
    return turns * (2.0 * math.pi / length)


def z_table(z_length):
    ang = angles(np.arange(z_length), np.arange(KZ), z_length)
    table = np.zeros((YB, z_length, 2, YB, KZ))
    for y in range(YB):
        table[y, :, 0, y] = np.cos(ang)
        table[y, :, 1, y] = -np.sin(ang)
    return table.reshape(YB * z_length, LB)


def y_table(blocks, cells, length, groups):
    per = KY // groups
    frequency = freq(KY)
    out = np.zeros((blocks, cells // YB, 2, YB, KZ, groups, LB))
    for b in range(blocks):
        ang = angles(b * cells + np.arange(cells), frequency, length)
        for y in range(cells):
            for j in range(KY):
                c, s = np.cos(ang[y, j]), np.sin(ang[y, j])
                for k in range(KZ):
                    re = (j % per) * KZ + k
                    im = per * KZ + re
                    at = (b, y // YB)
                    out[at + (0, y % YB, k, j // per, re)] = c
                    out[at + (1, y % YB, k, j // per, re)] = s
                    out[at + (0, y % YB, k, j // per, im)] = -s
                    out[at + (1, y % YB, k, j // per, im)] = c
    return out.reshape(blocks, cells // YB * LB, groups * LB)


def x_angles(blocks, cells, length):
    return angles(np.arange(blocks * cells), freq(KX), length).reshape(blocks, cells, KX)


def split(value):
    high = value.astype(BF16)
    return high, (value - high.astype(F32)).astype(BF16)


def mul(a, b):
    return jnp.dot(a, b, preferred_element_type=F32)


def tall(a):
    return jnp.concatenate([a[0], a[1], a[0]], axis=1)


def deep(a):
    return jnp.concatenate([a[0], a[1], a[0]], axis=0)


def wide(a):
    return jnp.concatenate([a[0], a[0], a[1]], axis=1)


def mul3(a, b):
    return mul(a[0], b[0]) + (mul(a[1], b[0]) + mul(a[0], b[1]))


def gelu(v):
    return (0.5 * v) * (1.0 + lax.erf(v * math.sqrt(0.5)))


def kernel(
    A, B, cells_x, scale1, scale2, gain,
    f_ref, lift_ref, lbias_ref, byp_ref, bi_ref, wo_ref, bo_ref, pr_ref, pb_ref,
    tzf_ref, tzi_ref, cs_ref, w1_hbm, w2_hbm, tx_hbm, yf1_hbm, yfc_hbm, yic_hbm, yi2_hbm,
    o_ref,
    w1, w2, tx, yf1, yfc, yic, yi2,
    buf1, r1, mx, mt1, ag1, yb1, ya1, zc, fx2, r2, buf2, r3, mt2, ag2, yb2, ya2, nar, yr1, yr2, pk_ref, fk_ref, t16, bd,
    csem, ssem, rsem,
):
    a = lax.axis_index("gx")
    b = lax.axis_index("gy")
    me = a * B + b
    IL = KX // A
    H = B // IL
    J = KY // H
    N = A * B
    CIN, C1 = lift_ref.shape
    C2 = wo_ref.shape[1]
    hx = cells_x // 2

    loads = [
        pltpu.make_async_copy(tx_hbm.at[a], tx, csem.at[0]),
        pltpu.make_async_copy(yf1_hbm.at[b], yf1, csem.at[1]),
        pltpu.make_async_copy(w1_hbm, w1, csem.at[2]),
        pltpu.make_async_copy(yic_hbm.at[b], yic, csem.at[3]),
        pltpu.make_async_copy(yfc_hbm.at[b], yfc, csem.at[4]),
        pltpu.make_async_copy(w2_hbm, w2, csem.at[5]),
        pltpu.make_async_copy(yi2_hbm.at[b], yi2, csem.at[6]),
    ]
    for load in loads:
        load.start()

    barrier = pltpu.get_barrier_semaphore()
    for step in range(1, N):
        peer = lax.rem(me + step, N)
        pl.semaphore_signal(
            barrier, inc=1, device_id=(peer // B, lax.rem(peer, B)), device_id_type=MESH
        )

    lane = lax.broadcasted_iota(jnp.int32, (1, LB), 1)
    sign_f = jnp.where(lane < LB // 2, 1.0, -1.0).astype(F32)

    def rot_f(v):
        return pltpu.roll(v, LB // 2, 1) * sign_f

    def rot_i(v):
        return pltpu.roll(v, LB // 2, 1) * -sign_f

    width = tzi_ref.shape[1]
    zs = []
    for ch in range(2):
        zs.append(mul(tall(split(f_ref[:, ch * width:(ch + 1) * width])), tzf_ref[...]))
    loads[0].wait()
    us = []
    for z in zs:
        us.append(mul3((tx[0], tx[1]), split(jnp.concatenate([z, rot_f(z)], axis=0))))
    loads[1].wait()
    part = mul3(split(jnp.concatenate(us, axis=1)), (yf1[0], yf1[1]))
    for i in range(KX):
        for h in range(H):
            buf1[i * H + h] = part[i * CIN:(i + 1) * CIN, h * LB:(h + 1) * LB]
    r1[me] = buf1[me]
    pl.semaphore_wait(barrier, N - 1)

    sends = []
    phase = []
    for step in range(1, N):
        peer = lax.rem(me + step, N)
        phase.append(pltpu.make_async_remote_copy(
            src_ref=buf1.at[peer], dst_ref=r1.at[me], send_sem=ssem.at[peer], recv_sem=rsem.at[me],
            device_id=(peer // B, lax.rem(peer, B)), device_id_type=MESH,
        ))
    for copy in phase:
        copy.start()
    sends += phase
    loads[2].wait()
    mx[...] = jnp.zeros_like(mx)
    mx[0:CIN, :C1] = lift_ref[...]
    mx[CIN:CIN + 1, :C1] = lbias_ref[...]
    mx[CIN + 1:CIN + 2, :C1] = bo_ref[...]
    lift8 = jnp.concatenate([mx[0:8, :C1]], axis=0)
    columns = mx[...].T[:C1]
    bo_col = columns[:, CIN + 1:CIN + 2]

    def left16(matrix, bias):
        n = matrix.shape[1]
        high, low = split(matrix[0:CIN])
        b0 = bias.astype(BF16)
        rest = bias - b0.astype(F32)
        b1 = rest.astype(BF16)
        b2 = (rest - b1.astype(F32)).astype(BF16)
        mx[...] = jnp.zeros_like(mx)
        mx[0:CIN, :n] = high.astype(F32)
        mx[CIN:2 * CIN, :n] = high.astype(F32)
        mx[2 * CIN:3 * CIN, :n] = low.astype(F32)
        for row, value in enumerate((b0, b1, b2)):
            mx[3 * CIN + row:3 * CIN + row + 1, :n] = value.astype(F32)
        return mx[...].T[:n, :16].astype(BF16)

    highest = lax.Precision.HIGHEST
    m = jnp.dot(lift8, byp_ref[...], precision=highest, preferred_element_type=F32)
    bp16 = left16(m, m[CIN:CIN + 1] + bi_ref[...])
    m = lax.dot_general(
        lift8, pr_ref[...], (((1,), (1,)), ((), ())), precision=highest, preferred_element_type=F32
    )
    pl16 = left16(m, m[CIN:CIN + 1] + pb_ref[...])
    t16[...] = jnp.ones_like(t16)

    def diagonal(value):
        rows, cols = value.shape
        bd[...] = jnp.zeros_like(bd)
        for g in range(GROUP):
            bd[g * rows:(g + 1) * rows, g * cols:(g + 1) * cols] = value
        return bd[0:GROUP * rows, 0:GROUP * cols]

    bp_bd = diagonal(bp16.astype(F32)).astype(BF16)
    pl_bd = diagonal(pl16.astype(F32)).astype(BF16)
    wo_bd = wide(split(diagonal(wo_ref[...])))
    pr_bd = wide(split(diagonal(pr_ref[...])))
    for step in range(1, N):
        peer = lax.rem(me + step, N)
        pltpu.make_async_remote_copy(
            src_ref=buf1.at[peer], dst_ref=r1.at[peer], send_sem=ssem.at[peer], recv_sem=rsem.at[peer],
            device_id=(peer // B, lax.rem(peer, B)), device_id_type=MESH,
        ).wait_recv()

    own = b // H
    gy_slot = [N, N + B, N + 2 * B]
    gx_slot = [N + 3 * B, N + 3 * B + KX, N + 3 * B + 2 * KX]

    def to_gy(source, target, slot, peer, index):
        return pltpu.make_async_remote_copy(
            src_ref=source, dst_ref=target.at[index], send_sem=ssem.at[gy_slot[slot] + peer],
            recv_sem=rsem.at[gy_slot[slot] + index], device_id=(a, peer), device_id_type=MESH,
        )

    def to_gx(source, target, slot, peer, index, il):
        return pltpu.make_async_remote_copy(
            src_ref=source, dst_ref=target.at[index, il],
            send_sem=ssem.at[gx_slot[slot] + peer * IL + il],
            recv_sem=rsem.at[gx_slot[slot] + index * IL + il],
            device_id=(peer, b), device_id_type=MESH,
        )

    def send(copy):
        copy.start()
        sends.append(copy)

    def gather(block, ag, slot):
        for step in range(1, B):
            peer = lax.rem(b + step, B)
            send(to_gy(block, ag, slot, peer, b))

    def expand(block, ag, table, yb, ya, slot, gx):
        for s in range(IL):
            il = lax.rem(own + s, IL)
            for t in range(1 if s == 0 else 0, H):
                source = il * H + lax.rem(b + t, H)
                to_gy(block, ag, slot, source, source).wait_recv()
            rows = jnp.concatenate([ag[il * H + h] for h in range(H)], axis=1)
            y = mul3(split(rows), (table[0], table[1]))
            yb[il] = y
            ya[a, il] = y
            for step in range(1, A):
                peer = lax.rem(a + step, A)
                send(to_gx(yb.at[il], ya, gx, peer, a, il))
        for s in range(IL):
            il = lax.rem(own + s, IL)
            for step in range(1, A):
                peer = lax.rem(a + step, A)
                to_gx(yb.at[il], ya, gx, peer, peer, il).wait_recv()

    def mix(st, w, width_out):
        mx[...] = jnp.zeros_like(mx)
        for j in range(J):
            for k in range(KZ):
                q = j * KZ + k
                p = J * KZ + q
                re = st[:, q:q + 1]
                im = st[:, p:p + 1]
                wr = w[j, 0, k]
                wi = w[j, 1, k]
                mx[q:q + 1, :width_out] = jnp.sum(re * wr - im * wi, axis=0, keepdims=True)
                mx[p:p + 1, :width_out] = jnp.sum(re * wi + im * wr, axis=0, keepdims=True)
        return mx[...].T[:width_out]

    s4 = jnp.sum(r1[...], axis=0) * scale1
    st = columns[:, 0:1] * s4[0:1]
    for c in range(1, CIN):
        st = st + columns[:, c:c + 1] * s4[c:c + 1]
    first = jnp.where((lane == 0) & (me == 0), gain, 0.0).astype(F32)
    st = st + columns[:, CIN:CIN + 1] * first
    mixed = mix(st, w1, C2)
    mt1[...] = mixed
    ag1[b] = mixed
    gather(mt1, ag1, 0)
    zn = width // YB

    def fill(value):
        n = value.shape[1]
        high, low = split(value)
        t16[0:CIN, :n] = high.astype(F32)
        t16[CIN:2 * CIN, :n] = low.astype(F32)
        t16[2 * CIN:3 * CIN, :n] = high.astype(F32)
        return t16[:, :n].astype(BF16)

    for x in range(hx):
        one = f_ref[2 * x * CIN:(2 * x + 1) * CIN]
        two = f_ref[(2 * x + 1) * CIN:(2 * x + 2) * CIN]
        fk_ref[2 * x] = fill(one)
        fk_ref[2 * x + 1] = fill(two)
        both = one + two
        pieces = [
            both[:, 2 * y * zn:(2 * y + 1) * zn] + both[:, (2 * y + 1) * zn:(2 * y + 2) * zn]
            for y in range(YB)
        ]
        pk_ref[x] = fill(jnp.concatenate(pieces, axis=1) * 0.25)
    loads[3].wait()
    expand(mt1, ag1, yic, yb1, ya1, 0, 0)
    for i in range(KX):
        yr1[i] = rot_i(ya1[i // IL, i % IL])

    HC = hx * KX

    def coarse_step(group, carry):
        parts = []
        for xx in range(GROUP):
            x = group * GROUP + xx
            acc = jnp.zeros((C2, LB), F32)
            for i in range(KX):
                c = cs_ref[a, x * KX + i]
                s = cs_ref[a, HC + x * KX + i]
                acc = acc + (c * ya1[i // IL, i % IL] + s * yr1[i])
            parts.append(acc)
        v = mul(tall(split(jnp.concatenate(parts, axis=0))), tzi_ref[...])
        near = jnp.concatenate([pk_ref[group * GROUP + xx] for xx in range(GROUP)], axis=0)
        g = split(gelu(v + mul(bp_bd, near)))
        narrow = mul(wo_bd, deep(g))
        wave = mul(tall(g), tzf_ref[...])
        for xx in range(GROUP):
            nar[group * GROUP + xx] = narrow[xx * C1:(xx + 1) * C1]
            zc[group * GROUP + xx] = wave[xx * C2:(xx + 1) * C2]
        return carry

    lax.fori_loop(0, hx // GROUP, coarse_step, 0)

    order = [lax.rem(own + 1 + s, IL) for s in range(IL)]
    for il in order:
        for t in range(A):
            peer = lax.rem(a + 1 + t, A)
            i = peer * IL + il
            re = jnp.zeros((C2, LB), F32)
            im = jnp.zeros((C2, LB), F32)
            for x in range(hx):
                re = re + cs_ref[a, x * KX + i] * zc[x]
                im = im + cs_ref[a, HC + x * KX + i] * zc[x]
            value = re + rot_f(im)
            if t < A - 1:
                fx2[peer, il] = value
                send(to_gx(fx2.at[peer, il], r2, 1, peer, a, il))
            else:
                r2[a, il] = value
    loads[4].wait()
    for s, il in enumerate(order):
        for step in range(1, A):
            peer = lax.rem(a + step, A)
            to_gx(fx2.at[peer, il], r2, 1, peer, peer, il).wait_recv()
        total = r2[0, il]
        for peer in range(1, A):
            total = total + r2[peer, il]
        out = mul3(split(total), (yfc[0], yfc[1]))
        for h in range(H):
            buf2[il * H + h] = out[:, h * LB:(h + 1) * LB]
        for t in range(1 if s == IL - 1 else 0, H):
            peer = il * H + lax.rem(b + t, H)
            send(to_gy(buf2.at[peer], r3, 1, peer, b))
    r3[b] = buf2[b]
    loads[5].wait()
    for step in range(1, B):
        peer = lax.rem(b + step, B)
        to_gy(buf2.at[peer], r3, 1, peer, peer).wait_recv()
    st = (jnp.sum(r3[...], axis=0) * scale2).T
    mixed = jnp.zeros((C1, LB), F32)
    for j in range(J):
        for k in range(KZ):
            q = j * KZ + k
            p = J * KZ + q
            re = st[q:q + 1]
            im = st[p:p + 1]
            wr = w2[j, 0, k]
            wi = w2[j, 1, k]
            real = jnp.sum(re * wr - im * wi, axis=1, keepdims=True)
            imag = jnp.sum(re * wi + im * wr, axis=1, keepdims=True)
            mixed = jnp.where(lane == q, real, jnp.where(lane == p, imag, mixed))
    mt2[...] = mixed
    ag2[b] = mixed
    gather(mt2, ag2, 2)
    loads[6].wait()
    expand(mt2, ag2, yi2, yb2, ya2, 2, 2)
    for i in range(KX):
        for ch in range(2):
            part = slice(ch * LB, (ch + 1) * LB)
            yr2[i, :, part] = rot_i(ya2[i // IL, i % IL, :, part])

    FC = cells_x * KX

    def fine_step(group, carry):
        parts = []
        for xx in range(GROUP):
            x = group * GROUP + xx
            acc = jnp.zeros((C1, 2 * LB), F32)
            for i in range(KX):
                c = cs_ref[a, 2 * HC + x * KX + i]
                s = cs_ref[a, 2 * HC + FC + x * KX + i]
                acc = acc + (c * ya2[i // IL, i % IL] + s * yr2[i])
            parts.append(acc)
        near = jnp.concatenate([fk_ref[group * GROUP + xx] for xx in range(GROUP)], axis=0)
        for ch in range(2):
            lines = jnp.concatenate([part[:, ch * LB:(ch + 1) * LB] for part in parts], axis=0)
            v = mul(tall(split(lines)), tzi_ref[...])
            rows = []
            for xx in range(0, GROUP, 2):
                half = nar.at[group * (GROUP // 2) + xx // 2]
                pieces = []
                for yy in range(YB):
                    at = (ch * YB + yy) // 2 * zn
                    pieces.append(half[:, at:at + zn])
                rows += [jnp.concatenate(pieces, axis=1) + bo_col] * 2
            g = split(gelu(v + jnp.concatenate(rows, axis=0)))
            cols = slice(ch * width, (ch + 1) * width)
            res = mul(pr_bd, deep(g)) + mul(pl_bd, near[:, cols])
            for xx in range(GROUP):
                o_ref[group * GROUP + xx, :, cols] = res[xx * CIN:(xx + 1) * CIN]
        return carry

    lax.fori_loop(0, cells_x // GROUP, fine_step, 0)
    for copy in sends:
        copy.wait_send()


def on_device(
    A, B, fields, lift, lift_bias, spectral_in, bypass_in, bias_in, spectral_out, bypass_out,
    bias_out, proj, proj_bias,
):
    cin, xc, yc, zc = fields.shape
    C1 = lift.shape[0]
    C2 = bypass_in.shape[0]
    NX = xc * A
    NY = yc * B
    IL = KX // A
    H = B // IL
    J = KY // H
    N = A * B
    width = YB * zc
    cells = float(NX * NY * zc)
    back = math.sqrt(2.0 / (KX * KY * KZ))

    tz = z_table(zc)
    tzf = stacked(tz)
    tzi = stacked(np.ascontiguousarray(tz.T) * back)
    fine_x = x_angles(A, xc, NX)
    half_x = x_angles(A, xc // 2, NX // 2)
    eye = np.eye(cin)
    tx = np.stack([
        np.concatenate([np.kron(np.cos(fine_x[i].T), eye), np.kron(np.sin(fine_x[i].T), eye)], axis=1)
        for i in range(A)
    ])
    cs = np.concatenate([
        np.cos(half_x).reshape(A, -1), np.sin(half_x).reshape(A, -1),
        np.cos(fine_x).reshape(A, -1), np.sin(fine_x).reshape(A, -1),
    ], axis=1).astype(np.float32)
    yf1 = y_table(B, yc, NY, H)
    yfc = y_table(B, yc // 2, NY // 2, H)

    def per_device(table):
        return jnp.asarray(np.ascontiguousarray(np.swapaxes(halves(table), 0, 1)))

    tx_t = per_device(tx)
    yf1_t = per_device(yf1)
    yfc_t = per_device(yfc)
    yic_t = per_device(np.swapaxes(yfc, 1, 2))
    yi2_t = per_device(np.swapaxes(yf1, 1, 2))

    rows = jnp.transpose(fields, (1, 0, 2, 3)).reshape(xc * cin, yc * zc)
    weights2 = jnp.swapaxes(spectral_out, 3, 4)

    vmem = pl.BlockSpec(memory_space=pltpu.VMEM)
    anywhere = pl.BlockSpec(memory_space=pl.ANY)
    V = pltpu.VMEM
    out = pl.pallas_call(
        functools.partial(
            kernel, A, B, xc, 1.0 / math.sqrt(cells), 1.0 / math.sqrt(cells / 4.0), math.sqrt(cells)
        ),
        out_shape=jax.ShapeDtypeStruct((xc, cin, yc * zc), F32),
        in_specs=[vmem] * 11 + [pl.BlockSpec(memory_space=pltpu.SMEM)] + [anywhere] * 7,
        out_specs=vmem,
        scratch_shapes=[
            V(spectral_in.shape, F32), V(weights2.shape, F32),
            V(tx_t.shape[1:], BF16), V(yf1_t.shape[1:], BF16), V(yfc_t.shape[1:], BF16),
            V(yic_t.shape[1:], BF16), V(yi2_t.shape[1:], BF16),
            V((N, cin, LB), F32), V((N, cin, LB), F32), V((LB, LB), F32),
            V((C2, LB), F32), V((B, C2, LB), F32),
            V((IL, C2, LB), F32), V((A, IL, C2, LB), F32),
            V((xc // 2, C2, LB), F32), V((A, IL, C2, LB), F32), V((A, IL, C2, LB), F32),
            V((B, C2, LB), F32), V((B, C2, LB), F32),
            V((C1, LB), F32), V((B, C1, LB), F32),
            V((IL, C1, 2 * LB), F32), V((A, IL, C1, 2 * LB), F32),
            V((xc // 2, C1, width), F32), V((KX, C2, LB), F32), V((KX, C1, 2 * LB), F32),
            V((xc // 2, 16, width), BF16), V((xc, 16, yc * zc), BF16), V((16, yc * zc), F32), V((GROUP * C2, GROUP * C2), F32),
            pltpu.SemaphoreType.DMA((7,)),
            pltpu.SemaphoreType.DMA((N + 3 * B + 3 * KX,)), pltpu.SemaphoreType.DMA((N + 3 * B + 3 * KX,)),
        ],
        compiler_params=pltpu.CompilerParams(
            collective_id=0, has_side_effects=True, vmem_limit_bytes=60 * 1024 * 1024
        ),
    )(
        rows, lift.T, lift_bias[None], bypass_in.T, bias_in[None], bypass_out, bias_out[None], proj,
        proj_bias[None], jnp.asarray(tzf), jnp.asarray(tzi),
        jnp.asarray(cs), spectral_in, weights2, tx_t, yf1_t, yfc_t, yic_t, yi2_t,
    )
    return jnp.transpose(out.reshape(xc, cin, yc, zc), (1, 0, 2, 3))


def solution(mesh):
    A = mesh.shape["gx"]
    B = mesh.shape["gy"]
    in_specs = (
        P(None, "gx", "gy", None), P(), P(), P(("gx", "gy"), None, None, None, None), P(), P(),
        P(("gx", "gy"), None, None, None, None), P(), P(), P(), P(),
    )
    return jax.shard_map(
        functools.partial(on_device, A, B), mesh=mesh, in_specs=in_specs,
        out_specs=P(None, "gx", "gy", None), check_vma=False,
    )
```

```python
import functools
import math

import jax
import jax.numpy as jnp
import numpy as np
from jax import lax
from jax.experimental import pallas as pl
from jax.experimental.pallas import tpu as pltpu
from jax.sharding import PartitionSpec as P

KX = 16
KY = 16
KZ = 8
YB = 8
LB = 128
GROUP = 4
F32 = jnp.float32
BF16 = jnp.bfloat16
MESH = pl.DeviceIdType.MESH


def freq(count):
    f = np.arange(count)
    return np.where(f < count // 2, f, f - count)


def halves(table):
    high = table.astype(np.float32).astype(jnp.bfloat16)
    low = (table - high.astype(np.float64)).astype(np.float32).astype(jnp.bfloat16)
    return np.stack([high, low])


def stacked(table):
    high, low = halves(table)
    return np.concatenate([high, high, low], axis=0)


def angles(places, frequency, length):
    turns = np.mod(places[:, None] * frequency[None, :], length)
    return turns * (2.0 * math.pi / length)


def z_table(z_length):
    ang = angles(np.arange(z_length), np.arange(KZ), z_length)
    table = np.zeros((YB, z_length, 2, YB, KZ))
    for y in range(YB):
        table[y, :, 0, y] = np.cos(ang)
        table[y, :, 1, y] = -np.sin(ang)
    return table.reshape(YB * z_length, LB)


def y_table(blocks, cells, length, groups):
    per = KY // groups
    frequency = freq(KY)
    out = np.zeros((blocks, cells // YB, 2, YB, KZ, groups, LB))
    for b in range(blocks):
        ang = angles(b * cells + np.arange(cells), frequency, length)
        for y in range(cells):
            for j in range(KY):
                c, s = np.cos(ang[y, j]), np.sin(ang[y, j])
                for k in range(KZ):
                    re = (j % per) * KZ + k
                    im = per * KZ + re
                    at = (b, y // YB)
                    out[at + (0, y % YB, k, j // per, re)] = c
                    out[at + (1, y % YB, k, j // per, re)] = s
                    out[at + (0, y % YB, k, j // per, im)] = -s
                    out[at + (1, y % YB, k, j // per, im)] = c
    return out.reshape(blocks, cells // YB * LB, groups * LB)


def x_angles(blocks, cells, length):
    return angles(np.arange(blocks * cells), freq(KX), length).reshape(blocks, cells, KX)


def split(value):
    high = value.astype(BF16)
    return high, (value - high.astype(F32)).astype(BF16)


def mul(a, b):
    return jnp.dot(a, b, preferred_element_type=F32)


def tall(a):
    return jnp.concatenate([a[0], a[1], a[0]], axis=1)


def deep(a):
    return jnp.concatenate([a[0], a[1], a[0]], axis=0)


def wide(a):
    return jnp.concatenate([a[0], a[0], a[1]], axis=1)


def mul3(a, b):
    return mul(a[0], b[0]) + (mul(a[1], b[0]) + mul(a[0], b[1]))


def gelu(v):
    return (0.5 * v) * (1.0 + lax.erf(v * math.sqrt(0.5)))


def kernel(
    A, B, cells_x, scale1, scale2, gain,
    f_ref, lift_ref, lbias_ref, byp_ref, bi_ref, wo_ref, bo_ref, pr_ref, pb_ref,
    tzf_ref, tzi_ref, cs_ref, w1_hbm, w2_hbm, tx_hbm, yf1_hbm, yfc_hbm, yic_hbm, yi2_hbm,
    o_ref,
    w1, w2, tx, yf1, yfc, yic, yi2,
    buf1, r1, mx, mt1, ag1, yb1, ya1, zc, fx2, r2, buf2, r3, mt2, ag2, yb2, ya2, nar, yr1, yr2, pk_ref, fk_ref, t16, bd,
    csem, ssem, rsem,
):
    a = lax.axis_index("gx")
    b = lax.axis_index("gy")
    me = a * B + b
    IL = KX // A
    H = B // IL
    J = KY // H
    N = A * B
    CIN, C1 = lift_ref.shape
    C2 = wo_ref.shape[1]
    hx = cells_x // 2

    loads = [
        pltpu.make_async_copy(tx_hbm.at[a], tx, csem.at[0]),
        pltpu.make_async_copy(yf1_hbm.at[b], yf1, csem.at[1]),
        pltpu.make_async_copy(w1_hbm, w1, csem.at[2]),
        pltpu.make_async_copy(yic_hbm.at[b], yic, csem.at[3]),
        pltpu.make_async_copy(yfc_hbm.at[b], yfc, csem.at[4]),
        pltpu.make_async_copy(w2_hbm, w2, csem.at[5]),
        pltpu.make_async_copy(yi2_hbm.at[b], yi2, csem.at[6]),
    ]
    for load in loads:
        load.start()

    barrier = pltpu.get_barrier_semaphore()
    for step in range(1, N):
        peer = lax.rem(me + step, N)
        pl.semaphore_signal(
            barrier, inc=1, device_id=(peer // B, lax.rem(peer, B)), device_id_type=MESH
        )

    lane = lax.broadcasted_iota(jnp.int32, (1, LB), 1)
    sign_f = jnp.where(lane < LB // 2, 1.0, -1.0).astype(F32)

    def rot_f(v):
        return pltpu.roll(v, LB // 2, 1) * sign_f

    def rot_i(v):
        return pltpu.roll(v, LB // 2, 1) * -sign_f

    width = tzi_ref.shape[1]
    zs = []
    for ch in range(2):
        zs.append(mul(tall(split(f_ref[:, ch * width:(ch + 1) * width])), tzf_ref[...]))
    loads[0].wait()
    us = []
    for z in zs:
        us.append(mul3((tx[0], tx[1]), split(jnp.concatenate([z, rot_f(z)], axis=0))))
    loads[1].wait()
    part = mul3(split(jnp.concatenate(us, axis=1)), (yf1[0], yf1[1]))
    for i in range(KX):
        for h in range(H):
            buf1[i * H + h] = part[i * CIN:(i + 1) * CIN, h * LB:(h + 1) * LB]
    r1[me] = buf1[me]
    pl.semaphore_wait(barrier, N - 1)

    sends = []
    phase = []
    for step in range(1, N):
        peer = lax.rem(me + step, N)
        phase.append(pltpu.make_async_remote_copy(
            src_ref=buf1.at[peer], dst_ref=r1.at[me], send_sem=ssem.at[peer], recv_sem=rsem.at[me],
            device_id=(peer // B, lax.rem(peer, B)), device_id_type=MESH,
        ))
    for copy in phase:
        copy.start()
    sends += phase
    loads[2].wait()
    mx[...] = jnp.zeros_like(mx)
    mx[0:CIN, :C1] = lift_ref[...]
    mx[CIN:CIN + 1, :C1] = lbias_ref[...]
    mx[CIN + 1:CIN + 2, :C1] = bo_ref[...]
    lift8 = jnp.concatenate([mx[0:8, :C1]], axis=0)
    columns = mx[...].T[:C1]
    bo_col = columns[:, CIN + 1:CIN + 2]

    def left16(matrix, bias):
        n = matrix.shape[1]
        high, low = split(matrix[0:CIN])
        b0 = bias.astype(BF16)
        rest = bias - b0.astype(F32)
        b1 = rest.astype(BF16)
        b2 = (rest - b1.astype(F32)).astype(BF16)
        mx[...] = jnp.zeros_like(mx)
        mx[0:CIN, :n] = high.astype(F32)
        mx[CIN:2 * CIN, :n] = high.astype(F32)
        mx[2 * CIN:3 * CIN, :n] = low.astype(F32)
        for row, value in enumerate((b0, b1, b2)):
            mx[3 * CIN + row:3 * CIN + row + 1, :n] = value.astype(F32)
        return mx[...].T[:n, :16].astype(BF16)

    highest = lax.Precision.HIGHEST
    m = jnp.dot(lift8, byp_ref[...], precision=highest, preferred_element_type=F32)
    bp16 = left16(m, m[CIN:CIN + 1] + bi_ref[...])
    m = lax.dot_general(
        lift8, pr_ref[...], (((1,), (1,)), ((), ())), precision=highest, preferred_element_type=F32
    )
    pl16 = left16(m, m[CIN:CIN + 1] + pb_ref[...])
    t16[...] = jnp.ones_like(t16)

    def diagonal(value):
        rows, cols = value.shape
        bd[...] = jnp.zeros_like(bd)
        for g in range(GROUP):
            bd[g * rows:(g + 1) * rows, g * cols:(g + 1) * cols] = value
        return bd[0:GROUP * rows, 0:GROUP * cols]

    bp_bd = diagonal(bp16.astype(F32)).astype(BF16)
    pl_bd = diagonal(pl16.astype(F32)).astype(BF16)
    wo_bd = wide(split(diagonal(wo_ref[...])))
    pr_bd = wide(split(diagonal(pr_ref[...])))
    for step in range(1, N):
        peer = lax.rem(me + step, N)
        pltpu.make_async_remote_copy(
            src_ref=buf1.at[peer], dst_ref=r1.at[peer], send_sem=ssem.at[peer], recv_sem=rsem.at[peer],
            device_id=(peer // B, lax.rem(peer, B)), device_id_type=MESH,
        ).wait_recv()

    own = b // H
    gy_slot = [N, N + B, N + 2 * B]
    gx_slot = [N + 3 * B, N + 3 * B + KX, N + 3 * B + 2 * KX]

    def to_gy(source, target, slot, peer, index):
        return pltpu.make_async_remote_copy(
            src_ref=source, dst_ref=target.at[index], send_sem=ssem.at[gy_slot[slot] + peer],
            recv_sem=rsem.at[gy_slot[slot] + index], device_id=(a, peer), device_id_type=MESH,
        )

    def to_gx(source, target, slot, peer, index, il):
        return pltpu.make_async_remote_copy(
            src_ref=source, dst_ref=target.at[index, il],
            send_sem=ssem.at[gx_slot[slot] + peer * IL + il],
            recv_sem=rsem.at[gx_slot[slot] + index * IL + il],
            device_id=(peer, b), device_id_type=MESH,
        )

    def send(copy):
        copy.start()
        sends.append(copy)

    Q = B // 4 if B % 4 == 0 and H % (B // 4) == 0 else 1
    R = H // Q
    plane = b // Q
    column = lax.rem(b, Q)
    core = lax.rem(a, 2)
    partner = a + 1 - 2 * core

    def gather(block, ag, slot):
        for step in range(1, B // Q):
            send(to_gy(block, ag, slot, lax.rem(plane + step, B // Q) * Q + column, b))
        for step in range(1, Q):
            send(to_gy(block, ag, slot, plane * Q + lax.rem(column + step, Q), b))

    def expand(block, ag, table, yb, ya, slot, gx):
        def planes(s):
            il = lax.rem(own + s, IL)
            return il, [il * R + lax.rem(plane + r, R) for r in range(R)]

        def relay(s):
            for r, place in enumerate(planes(s)[1]):
                if s == 0 and r == 0:
                    continue
                source = place * Q + column
                to_gy(block, ag, slot, source, source).wait_recv()
                for step in range(1, Q):
                    other = lax.rem(column + step, Q)
                    copy = pltpu.make_async_remote_copy(
                        src_ref=ag.at[source], dst_ref=ag.at[source],
                        send_sem=ssem.at[gy_slot[slot] + place * Q + other],
                        recv_sem=rsem.at[gy_slot[slot] + source],
                        device_id=(a, plane * Q + other), device_id_type=MESH,
                    )
                    send(copy)

        def process(s):
            il, places = planes(s)
            for place in places:
                for step in range(1, Q):
                    source = place * Q + lax.rem(column + step, Q)
                    to_gy(block, ag, slot, source, source).wait_recv()
            rows = jnp.concatenate([ag[il * H + h] for h in range(H)], axis=1)
            y = mul3(split(rows), (table[0], table[1]))
            yb[il] = y
            ya[a, il] = y
            for step in range(1, A // 2):
                send(to_gx(yb.at[il], ya, gx, lax.rem(a + 2 * step, A), a, il))
            send(to_gx(yb.at[il], ya, gx, partner, a, il))

        def across(s):
            il = lax.rem(own + s, IL)
            for step in range(1, A // 2):
                peer = lax.rem(a + 2 * step, A)
                to_gx(yb.at[il], ya, gx, peer, peer, il).wait_recv()
                twin = peer + 1 - 2 * core
                copy = pltpu.make_async_remote_copy(
                    src_ref=ya.at[peer, il], dst_ref=ya.at[peer, il],
                    send_sem=ssem.at[gx_slot[gx] + twin * IL + il],
                    recv_sem=rsem.at[gx_slot[gx] + peer * IL + il],
                    device_id=(partner, b), device_id_type=MESH,
                )
                send(copy)

        relay(0)
        for s in range(IL):
            if s + 1 < IL:
                relay(s + 1)
            process(s)
            if s >= 1:
                across(s - 1)
        across(IL - 1)
        for s in range(IL):
            il = lax.rem(own + s, IL)
            for step in range(0, A // 2):
                peer = lax.rem(partner + 2 * step, A)
                to_gx(yb.at[il], ya, gx, peer, peer, il).wait_recv()

    def mix(st, w, width_out):
        mx[...] = jnp.zeros_like(mx)
        for j in range(J):
            for k in range(KZ):
                q = j * KZ + k
                p = J * KZ + q
                re = st[:, q:q + 1]
                im = st[:, p:p + 1]
                wr = w[j, 0, k]
                wi = w[j, 1, k]
                mx[q:q + 1, :width_out] = jnp.sum(re * wr - im * wi, axis=0, keepdims=True)
                mx[p:p + 1, :width_out] = jnp.sum(re * wi + im * wr, axis=0, keepdims=True)
        return mx[...].T[:width_out]

    s4 = jnp.sum(r1[...], axis=0) * scale1
    st = columns[:, 0:1] * s4[0:1]
    for c in range(1, CIN):
        st = st + columns[:, c:c + 1] * s4[c:c + 1]
    first = jnp.where((lane == 0) & (me == 0), gain, 0.0).astype(F32)
    st = st + columns[:, CIN:CIN + 1] * first
    mixed = mix(st, w1, C2)
    mt1[...] = mixed
    ag1[b] = mixed
    gather(mt1, ag1, 0)
    zn = width // YB

    def fill(value):
        n = value.shape[1]
        high, low = split(value)
        t16[0:CIN, :n] = high.astype(F32)
        t16[CIN:2 * CIN, :n] = low.astype(F32)
        t16[2 * CIN:3 * CIN, :n] = high.astype(F32)
        return t16[:, :n].astype(BF16)

    for x in range(hx):
        one = f_ref[2 * x * CIN:(2 * x + 1) * CIN]
        two = f_ref[(2 * x + 1) * CIN:(2 * x + 2) * CIN]
        fk_ref[2 * x] = fill(one)
        fk_ref[2 * x + 1] = fill(two)
        both = one + two
        pieces = [
            both[:, 2 * y * zn:(2 * y + 1) * zn] + both[:, (2 * y + 1) * zn:(2 * y + 2) * zn]
            for y in range(YB)
        ]
        pk_ref[x] = fill(jnp.concatenate(pieces, axis=1) * 0.25)
    loads[3].wait()
    expand(mt1, ag1, yic, yb1, ya1, 0, 0)
    for i in range(KX):
        yr1[i] = rot_i(ya1[i // IL, i % IL])

    HC = hx * KX

    def coarse_step(group, carry):
        parts = []
        for xx in range(GROUP):
            x = group * GROUP + xx
            acc = jnp.zeros((C2, LB), F32)
            for i in range(KX):
                c = cs_ref[a, x * KX + i]
                s = cs_ref[a, HC + x * KX + i]
                acc = acc + (c * ya1[i // IL, i % IL] + s * yr1[i])
            parts.append(acc)
        v = mul(tall(split(jnp.concatenate(parts, axis=0))), tzi_ref[...])
        near = jnp.concatenate([pk_ref[group * GROUP + xx] for xx in range(GROUP)], axis=0)
        g = split(gelu(v + mul(bp_bd, near)))
        narrow = mul(wo_bd, deep(g))
        wave = mul(tall(g), tzf_ref[...])
        for xx in range(GROUP):
            nar[group * GROUP + xx] = narrow[xx * C1:(xx + 1) * C1]
            zc[group * GROUP + xx] = wave[xx * C2:(xx + 1) * C2]
        return carry

    lax.fori_loop(0, hx // GROUP, coarse_step, 0)

    order = [lax.rem(own + 1 + s, IL) for s in range(IL)]
    for il in order:
        for t in range(A):
            peer = lax.rem(a + 1 + t, A)
            i = peer * IL + il
            re = jnp.zeros((C2, LB), F32)
            im = jnp.zeros((C2, LB), F32)
            for x in range(hx):
                re = re + cs_ref[a, x * KX + i] * zc[x]
                im = im + cs_ref[a, HC + x * KX + i] * zc[x]
            value = re + rot_f(im)
            if t < A - 1:
                fx2[peer, il] = value
                send(to_gx(fx2.at[peer, il], r2, 1, peer, a, il))
            else:
                r2[a, il] = value
    loads[4].wait()
    for s, il in enumerate(order):
        for step in range(1, A):
            peer = lax.rem(a + step, A)
            to_gx(fx2.at[peer, il], r2, 1, peer, peer, il).wait_recv()
        total = r2[0, il]
        for peer in range(1, A):
            total = total + r2[peer, il]
        out = mul3(split(total), (yfc[0], yfc[1]))
        for h in range(H):
            buf2[il * H + h] = out[:, h * LB:(h + 1) * LB]
        for t in range(1 if s == IL - 1 else 0, H):
            peer = il * H + lax.rem(b + t, H)
            send(to_gy(buf2.at[peer], r3, 1, peer, b))
    r3[b] = buf2[b]
    loads[5].wait()
    for step in range(1, B):
        peer = lax.rem(b + step, B)
        to_gy(buf2.at[peer], r3, 1, peer, peer).wait_recv()
    st = (jnp.sum(r3[...], axis=0) * scale2).T
    mixed = jnp.zeros((C1, LB), F32)
    for j in range(J):
        for k in range(KZ):
            q = j * KZ + k
            p = J * KZ + q
            re = st[q:q + 1]
            im = st[p:p + 1]
            wr = w2[j, 0, k]
            wi = w2[j, 1, k]
            real = jnp.sum(re * wr - im * wi, axis=1, keepdims=True)
            imag = jnp.sum(re * wi + im * wr, axis=1, keepdims=True)
            mixed = jnp.where(lane == q, real, jnp.where(lane == p, imag, mixed))
    mt2[...] = mixed
    ag2[b] = mixed
    gather(mt2, ag2, 2)
    loads[6].wait()
    expand(mt2, ag2, yi2, yb2, ya2, 2, 2)
    for i in range(KX):
        for ch in range(2):
            part = slice(ch * LB, (ch + 1) * LB)
            yr2[i, :, part] = rot_i(ya2[i // IL, i % IL, :, part])

    FC = cells_x * KX

    def fine_step(group, carry):
        parts = []
        for xx in range(GROUP):
            x = group * GROUP + xx
            acc = jnp.zeros((C1, 2 * LB), F32)
            for i in range(KX):
                c = cs_ref[a, 2 * HC + x * KX + i]
                s = cs_ref[a, 2 * HC + FC + x * KX + i]
                acc = acc + (c * ya2[i // IL, i % IL] + s * yr2[i])
            parts.append(acc)
        near = jnp.concatenate([fk_ref[group * GROUP + xx] for xx in range(GROUP)], axis=0)
        for ch in range(2):
            lines = jnp.concatenate([part[:, ch * LB:(ch + 1) * LB] for part in parts], axis=0)
            v = mul(tall(split(lines)), tzi_ref[...])
            rows = []
            for xx in range(0, GROUP, 2):
                half = nar.at[group * (GROUP // 2) + xx // 2]
                pieces = []
                for yy in range(YB):
                    at = (ch * YB + yy) // 2 * zn
                    pieces.append(half[:, at:at + zn])
                rows += [jnp.concatenate(pieces, axis=1) + bo_col] * 2
            g = split(gelu(v + jnp.concatenate(rows, axis=0)))
            cols = slice(ch * width, (ch + 1) * width)
            res = mul(pr_bd, deep(g)) + mul(pl_bd, near[:, cols])
            for xx in range(GROUP):
                o_ref[group * GROUP + xx, :, cols] = res[xx * CIN:(xx + 1) * CIN]
        return carry

    lax.fori_loop(0, cells_x // GROUP, fine_step, 0)
    for copy in sends:
        copy.wait_send()


def on_device(
    A, B, fields, lift, lift_bias, spectral_in, bypass_in, bias_in, spectral_out, bypass_out,
    bias_out, proj, proj_bias,
):
    cin, xc, yc, zc = fields.shape
    C1 = lift.shape[0]
    C2 = bypass_in.shape[0]
    NX = xc * A
    NY = yc * B
    IL = KX // A
    H = B // IL
    J = KY // H
    N = A * B
    width = YB * zc
    cells = float(NX * NY * zc)
    back = math.sqrt(2.0 / (KX * KY * KZ))

    tz = z_table(zc)
    tzf = stacked(tz)
    tzi = stacked(np.ascontiguousarray(tz.T) * back)
    fine_x = x_angles(A, xc, NX)
    half_x = x_angles(A, xc // 2, NX // 2)
    eye = np.eye(cin)
    tx = np.stack([
        np.concatenate([np.kron(np.cos(fine_x[i].T), eye), np.kron(np.sin(fine_x[i].T), eye)], axis=1)
        for i in range(A)
    ])
    cs = np.concatenate([
        np.cos(half_x).reshape(A, -1), np.sin(half_x).reshape(A, -1),
        np.cos(fine_x).reshape(A, -1), np.sin(fine_x).reshape(A, -1),
    ], axis=1).astype(np.float32)
    yf1 = y_table(B, yc, NY, H)
    yfc = y_table(B, yc // 2, NY // 2, H)

    def per_device(table):
        return jnp.asarray(np.ascontiguousarray(np.swapaxes(halves(table), 0, 1)))

    tx_t = per_device(tx)
    yf1_t = per_device(yf1)
    yfc_t = per_device(yfc)
    yic_t = per_device(np.swapaxes(yfc, 1, 2))
    yi2_t = per_device(np.swapaxes(yf1, 1, 2))

    rows = jnp.transpose(fields, (1, 0, 2, 3)).reshape(xc * cin, yc * zc)
    weights2 = jnp.swapaxes(spectral_out, 3, 4)

    vmem = pl.BlockSpec(memory_space=pltpu.VMEM)
    anywhere = pl.BlockSpec(memory_space=pl.ANY)
    V = pltpu.VMEM
    out = pl.pallas_call(
        functools.partial(
            kernel, A, B, xc, 1.0 / math.sqrt(cells), 1.0 / math.sqrt(cells / 4.0), math.sqrt(cells)
        ),
        out_shape=jax.ShapeDtypeStruct((xc, cin, yc * zc), F32),
        in_specs=[vmem] * 11 + [pl.BlockSpec(memory_space=pltpu.SMEM)] + [anywhere] * 7,
        out_specs=vmem,
        scratch_shapes=[
            V(spectral_in.shape, F32), V(weights2.shape, F32),
            V(tx_t.shape[1:], BF16), V(yf1_t.shape[1:], BF16), V(yfc_t.shape[1:], BF16),
            V(yic_t.shape[1:], BF16), V(yi2_t.shape[1:], BF16),
            V((N, cin, LB), F32), V((N, cin, LB), F32), V((LB, LB), F32),
            V((C2, LB), F32), V((B, C2, LB), F32),
            V((IL, C2, LB), F32), V((A, IL, C2, LB), F32),
            V((xc // 2, C2, LB), F32), V((A, IL, C2, LB), F32), V((A, IL, C2, LB), F32),
            V((B, C2, LB), F32), V((B, C2, LB), F32),
            V((C1, LB), F32), V((B, C1, LB), F32),
            V((IL, C1, 2 * LB), F32), V((A, IL, C1, 2 * LB), F32),
            V((xc // 2, C1, width), F32), V((KX, C2, LB), F32), V((KX, C1, 2 * LB), F32),
            V((xc // 2, 16, width), BF16), V((xc, 16, yc * zc), BF16), V((16, yc * zc), F32), V((GROUP * C2, GROUP * C2), F32),
            pltpu.SemaphoreType.DMA((7,)),
            pltpu.SemaphoreType.DMA((N + 3 * B + 3 * KX,)), pltpu.SemaphoreType.DMA((N + 3 * B + 3 * KX,)),
        ],
        compiler_params=pltpu.CompilerParams(
            collective_id=0, has_side_effects=True, vmem_limit_bytes=60 * 1024 * 1024
        ),
    )(
        rows, lift.T, lift_bias[None], bypass_in.T, bias_in[None], bypass_out, bias_out[None], proj,
        proj_bias[None], jnp.asarray(tzf), jnp.asarray(tzi),
        jnp.asarray(cs), spectral_in, weights2, tx_t, yf1_t, yfc_t, yic_t, yi2_t,
    )
    return jnp.transpose(out.reshape(xc, cin, yc, zc), (1, 0, 2, 3))


def solution(mesh):
    A = mesh.shape["gx"]
    B = mesh.shape["gy"]
    in_specs = (
        P(None, "gx", "gy", None), P(), P(), P(("gx", "gy"), None, None, None, None), P(), P(),
        P(("gx", "gy"), None, None, None, None), P(), P(), P(), P(),
    )
    return jax.shard_map(
        functools.partial(on_device, A, B), mesh=mesh, in_specs=in_specs,
        out_specs=P(None, "gx", "gy", None), check_vma=False,
    )
```

```python
import functools
import math

import jax
import jax.numpy as jnp
import numpy as np
from jax import lax
from jax.experimental import pallas as pl
from jax.experimental.pallas import tpu as pltpu
from jax.sharding import PartitionSpec as P

KX = 16
KY = 16
KZ = 8
YB = 8
LB = 128
GROUP = 4
F32 = jnp.float32
BF16 = jnp.bfloat16
MESH = pl.DeviceIdType.MESH


def freq(count):
    f = np.arange(count)
    return np.where(f < count // 2, f, f - count)


def halves(table):
    high = table.astype(np.float32).astype(jnp.bfloat16)
    low = (table - high.astype(np.float64)).astype(np.float32).astype(jnp.bfloat16)
    return np.stack([high, low])


def stacked(table):
    high, low = halves(table)
    return np.concatenate([high, high, low], axis=0)


def angles(places, frequency, length):
    turns = np.mod(places[:, None] * frequency[None, :], length)
    return turns * (2.0 * math.pi / length)


def z_table(z_length):
    ang = angles(np.arange(z_length), np.arange(KZ), z_length)
    table = np.zeros((YB, z_length, 2, YB, KZ))
    for y in range(YB):
        table[y, :, 0, y] = np.cos(ang)
        table[y, :, 1, y] = -np.sin(ang)
    return table.reshape(YB * z_length, LB)


def y_table(blocks, cells, length, groups):
    per = KY // groups
    frequency = freq(KY)
    out = np.zeros((blocks, cells // YB, 2, YB, KZ, groups, LB))
    for b in range(blocks):
        ang = angles(b * cells + np.arange(cells), frequency, length)
        for y in range(cells):
            for j in range(KY):
                c, s = np.cos(ang[y, j]), np.sin(ang[y, j])
                for k in range(KZ):
                    re = (j % per) * KZ + k
                    im = per * KZ + re
                    at = (b, y // YB)
                    out[at + (0, y % YB, k, j // per, re)] = c
                    out[at + (1, y % YB, k, j // per, re)] = s
                    out[at + (0, y % YB, k, j // per, im)] = -s
                    out[at + (1, y % YB, k, j // per, im)] = c
    return out.reshape(blocks, cells // YB * LB, groups * LB)


def x_angles(blocks, cells, length):
    return angles(np.arange(blocks * cells), freq(KX), length).reshape(blocks, cells, KX)


def split(value):
    high = value.astype(BF16)
    return high, (value - high.astype(F32)).astype(BF16)


def mul(a, b):
    return jnp.dot(a, b, preferred_element_type=F32)


def tall(a):
    return jnp.concatenate([a[0], a[1], a[0]], axis=1)


def deep(a):
    return jnp.concatenate([a[0], a[1], a[0]], axis=0)


def wide(a):
    return jnp.concatenate([a[0], a[0], a[1]], axis=1)


def mul3(a, b):
    return mul(a[0], b[0]) + (mul(a[1], b[0]) + mul(a[0], b[1]))


def gelu(v):
    return (0.5 * v) * (1.0 + lax.erf(v * math.sqrt(0.5)))


def kernel(
    A, B, cells_x, scale1, scale2, gain,
    f_ref, lift_ref, lbias_ref, byp_ref, bi_ref, wo_ref, bo_ref, pr_ref, pb_ref,
    tzf_ref, cs_ref, tzi_hbm, w1_hbm, w2_hbm, tx_hbm, yf1_hbm, yfc_hbm, yic_hbm, yi2_hbm,
    o_ref,
    tzi_ref, w1, w2, tx, yf1, yfc, yic, yi2,
    buf1, r1, mx, mt1, ag1, yb1, ya1, zc, fx2, r2, buf2, r3, mt2, ag2, yb2, ya2, nar, yr1, yr2, pk_ref, fk_ref, t16, bd,
    csem, ssem, rsem,
):
    a = lax.axis_index("gx")
    b = lax.axis_index("gy")
    me = a * B + b
    IL = KX // A
    H = B // IL
    J = KY // H
    N = A * B
    CIN, C1 = lift_ref.shape
    C2 = wo_ref.shape[1]
    hx = cells_x // 2

    loads = [
        pltpu.make_async_copy(tx_hbm.at[a], tx, csem.at[0]),
        pltpu.make_async_copy(yf1_hbm.at[b], yf1, csem.at[1]),
        pltpu.make_async_copy(w1_hbm, w1, csem.at[2]),
        pltpu.make_async_copy(yic_hbm.at[b], yic, csem.at[3]),
        pltpu.make_async_copy(yfc_hbm.at[b], yfc, csem.at[4]),
        pltpu.make_async_copy(w2_hbm, w2, csem.at[5]),
        pltpu.make_async_copy(yi2_hbm.at[b], yi2, csem.at[6]),
        pltpu.make_async_copy(tzi_hbm, tzi_ref, csem.at[7]),
    ]
    for load in loads:
        load.start()

    barrier = pltpu.get_barrier_semaphore()
    for step in range(1, N):
        peer = lax.rem(me + step, N)
        pl.semaphore_signal(
            barrier, inc=1, device_id=(peer // B, lax.rem(peer, B)), device_id_type=MESH
        )

    lane = lax.broadcasted_iota(jnp.int32, (1, LB), 1)
    sign_f = jnp.where(lane < LB // 2, 1.0, -1.0).astype(F32)

    def rot_f(v):
        return pltpu.roll(v, LB // 2, 1) * sign_f

    def rot_i(v):
        return pltpu.roll(v, LB // 2, 1) * -sign_f

    width = tzi_ref.shape[1]
    zs = []
    for ch in range(2):
        zs.append(mul(tall(split(f_ref[:, ch * width:(ch + 1) * width])), tzf_ref[...]))
    loads[0].wait()
    us = []
    for z in zs:
        us.append(mul3((tx[0], tx[1]), split(jnp.concatenate([z, rot_f(z)], axis=0))))
    loads[1].wait()
    part = mul3(split(jnp.concatenate(us, axis=1)), (yf1[0], yf1[1]))
    for i in range(KX):
        for h in range(H):
            buf1[i * H + h] = part[i * CIN:(i + 1) * CIN, h * LB:(h + 1) * LB]
    r1[me] = buf1[me]
    pl.semaphore_wait(barrier, N - 1)

    sends = []
    phase = []
    for step in range(1, N):
        peer = lax.rem(me + step, N)
        phase.append(pltpu.make_async_remote_copy(
            src_ref=buf1.at[peer], dst_ref=r1.at[me], send_sem=ssem.at[peer], recv_sem=rsem.at[me],
            device_id=(peer // B, lax.rem(peer, B)), device_id_type=MESH,
        ))
    for copy in phase:
        copy.start()
    sends += phase
    loads[2].wait()
    mx[...] = jnp.zeros_like(mx)
    mx[0:CIN, :C1] = lift_ref[...]
    mx[CIN:CIN + 1, :C1] = lbias_ref[...]
    mx[CIN + 1:CIN + 2, :C1] = bo_ref[...]
    lift8 = jnp.concatenate([mx[0:8, :C1]], axis=0)
    columns = mx[...].T[:C1]
    bo_col = columns[:, CIN + 1:CIN + 2]

    def left16(matrix, bias):
        n = matrix.shape[1]
        high, low = split(matrix[0:CIN])
        b0 = bias.astype(BF16)
        rest = bias - b0.astype(F32)
        b1 = rest.astype(BF16)
        b2 = (rest - b1.astype(F32)).astype(BF16)
        mx[...] = jnp.zeros_like(mx)
        mx[0:CIN, :n] = high.astype(F32)
        mx[CIN:2 * CIN, :n] = high.astype(F32)
        mx[2 * CIN:3 * CIN, :n] = low.astype(F32)
        for row, value in enumerate((b0, b1, b2)):
            mx[3 * CIN + row:3 * CIN + row + 1, :n] = value.astype(F32)
        return mx[...].T[:n, :16].astype(BF16)

    highest = lax.Precision.HIGHEST
    m = jnp.dot(lift8, byp_ref[...], precision=highest, preferred_element_type=F32)
    bp16 = left16(m, m[CIN:CIN + 1] + bi_ref[...])
    m = lax.dot_general(
        lift8, pr_ref[...], (((1,), (1,)), ((), ())), precision=highest, preferred_element_type=F32
    )
    pl16 = left16(m, m[CIN:CIN + 1] + pb_ref[...])
    t16[...] = jnp.ones_like(t16)

    def diagonal(value):
        rows, cols = value.shape
        bd[...] = jnp.zeros_like(bd)
        for g in range(GROUP):
            bd[g * rows:(g + 1) * rows, g * cols:(g + 1) * cols] = value
        return bd[0:GROUP * rows, 0:GROUP * cols]

    bp_bd = diagonal(bp16.astype(F32)).astype(BF16)
    pl_bd = diagonal(pl16.astype(F32)).astype(BF16)
    wo_bd = wide(split(diagonal(wo_ref[...])))
    pr_bd = wide(split(diagonal(pr_ref[...])))
    for step in range(1, N):
        peer = lax.rem(me + step, N)
        pltpu.make_async_remote_copy(
            src_ref=buf1.at[peer], dst_ref=r1.at[peer], send_sem=ssem.at[peer], recv_sem=rsem.at[peer],
            device_id=(peer // B, lax.rem(peer, B)), device_id_type=MESH,
        ).wait_recv()

    own = b // H
    gy_slot = [N, N + B, N + 2 * B]
    gx_slot = [N + 3 * B, N + 3 * B + KX, N + 3 * B + 2 * KX]

    def to_gy(source, target, slot, peer, index):
        return pltpu.make_async_remote_copy(
            src_ref=source, dst_ref=target.at[index], send_sem=ssem.at[gy_slot[slot] + peer],
            recv_sem=rsem.at[gy_slot[slot] + index], device_id=(a, peer), device_id_type=MESH,
        )

    def to_gx(source, target, slot, peer, index, il):
        return pltpu.make_async_remote_copy(
            src_ref=source, dst_ref=target.at[index, il],
            send_sem=ssem.at[gx_slot[slot] + peer * IL + il],
            recv_sem=rsem.at[gx_slot[slot] + index * IL + il],
            device_id=(peer, b), device_id_type=MESH,
        )

    def send(copy):
        copy.start()
        sends.append(copy)

    def gather(block, ag, slot):
        for step in range(1, B):
            peer = lax.rem(b + step, B)
            send(to_gy(block, ag, slot, peer, b))

    def expand(block, ag, table, yb, ya, slot, gx):
        for s in range(IL):
            il = lax.rem(own + s, IL)
            for t in range(1 if s == 0 else 0, H):
                source = il * H + lax.rem(b + t, H)
                to_gy(block, ag, slot, source, source).wait_recv()
            rows = jnp.concatenate([ag[il * H + h] for h in range(H)], axis=1)
            y = mul3(split(rows), (table[0], table[1]))
            yb[il] = y
            ya[a, il] = y
            for step in range(1, A):
                peer = lax.rem(a + step, A)
                send(to_gx(yb.at[il], ya, gx, peer, a, il))
        for s in range(IL):
            il = lax.rem(own + s, IL)
            for step in range(1, A):
                peer = lax.rem(a + step, A)
                to_gx(yb.at[il], ya, gx, peer, peer, il).wait_recv()

    def mix(st, w, width_out):
        mx[...] = jnp.zeros_like(mx)
        for j in range(J):
            for k in range(KZ):
                q = j * KZ + k
                p = J * KZ + q
                re = st[:, q:q + 1]
                im = st[:, p:p + 1]
                wr = w[j, 0, k]
                wi = w[j, 1, k]
                mx[q:q + 1, :width_out] = jnp.sum(re * wr - im * wi, axis=0, keepdims=True)
                mx[p:p + 1, :width_out] = jnp.sum(re * wi + im * wr, axis=0, keepdims=True)
        return mx[...].T[:width_out]

    s4 = jnp.sum(r1[...], axis=0) * scale1
    st = columns[:, 0:1] * s4[0:1]
    for c in range(1, CIN):
        st = st + columns[:, c:c + 1] * s4[c:c + 1]
    first = jnp.where((lane == 0) & (me == 0), gain, 0.0).astype(F32)
    st = st + columns[:, CIN:CIN + 1] * first
    mixed = mix(st, w1, C2)
    mt1[...] = mixed
    ag1[b] = mixed
    gather(mt1, ag1, 0)
    zn = width // YB

    def fill(value):
        n = value.shape[1]
        high, low = split(value)
        t16[0:CIN, :n] = high.astype(F32)
        t16[CIN:2 * CIN, :n] = low.astype(F32)
        t16[2 * CIN:3 * CIN, :n] = high.astype(F32)
        return t16[:, :n].astype(BF16)

    for x in range(hx):
        one = f_ref[2 * x * CIN:(2 * x + 1) * CIN]
        two = f_ref[(2 * x + 1) * CIN:(2 * x + 2) * CIN]
        fk_ref[2 * x] = fill(one)
        fk_ref[2 * x + 1] = fill(two)
        both = one + two
        pieces = [
            both[:, 2 * y * zn:(2 * y + 1) * zn] + both[:, (2 * y + 1) * zn:(2 * y + 2) * zn]
            for y in range(YB)
        ]
        pk_ref[x] = fill(jnp.concatenate(pieces, axis=1) * 0.25)
    loads[3].wait()
    expand(mt1, ag1, yic, yb1, ya1, 0, 0)
    for i in range(KX):
        yr1[i] = rot_i(ya1[i // IL, i % IL])

    HC = hx * KX

    def coarse_step(group, carry):
        parts = []
        for xx in range(GROUP):
            x = group * GROUP + xx
            acc = jnp.zeros((C2, LB), F32)
            for i in range(KX):
                c = cs_ref[a, x * KX + i]
                s = cs_ref[a, HC + x * KX + i]
                acc = acc + (c * ya1[i // IL, i % IL] + s * yr1[i])
            parts.append(acc)
        v = mul(tall(split(jnp.concatenate(parts, axis=0))), tzi_ref[...])
        near = jnp.concatenate([pk_ref[group * GROUP + xx] for xx in range(GROUP)], axis=0)
        g = split(gelu(v + mul(bp_bd, near)))
        narrow = mul(wo_bd, deep(g))
        wave = mul(tall(g), tzf_ref[...])
        for xx in range(GROUP):
            nar[group * GROUP + xx] = narrow[xx * C1:(xx + 1) * C1]
            zc[group * GROUP + xx] = wave[xx * C2:(xx + 1) * C2]
        return carry

    loads[7].wait()
    lax.fori_loop(0, hx // GROUP, coarse_step, 0)

    order = [lax.rem(own + 1 + s, IL) for s in range(IL)]
    for il in order:
        for t in range(A):
            peer = lax.rem(a + 1 + t, A)
            i = peer * IL + il
            re = jnp.zeros((C2, LB), F32)
            im = jnp.zeros((C2, LB), F32)
            for x in range(hx):
                re = re + cs_ref[a, x * KX + i] * zc[x]
                im = im + cs_ref[a, HC + x * KX + i] * zc[x]
            value = re + rot_f(im)
            if t < A - 1:
                fx2[peer, il] = value
                send(to_gx(fx2.at[peer, il], r2, 1, peer, a, il))
            else:
                r2[a, il] = value
    loads[4].wait()
    for s, il in enumerate(order):
        for step in range(1, A):
            peer = lax.rem(a + step, A)
            to_gx(fx2.at[peer, il], r2, 1, peer, peer, il).wait_recv()
        total = r2[0, il]
        for peer in range(1, A):
            total = total + r2[peer, il]
        out = mul3(split(total), (yfc[0], yfc[1]))
        for h in range(H):
            buf2[il * H + h] = out[:, h * LB:(h + 1) * LB]
        for t in range(1 if s == IL - 1 else 0, H):
            peer = il * H + lax.rem(b + t, H)
            send(to_gy(buf2.at[peer], r3, 1, peer, b))
    r3[b] = buf2[b]
    loads[5].wait()
    for step in range(1, B):
        peer = lax.rem(b + step, B)
        to_gy(buf2.at[peer], r3, 1, peer, peer).wait_recv()
    st = (jnp.sum(r3[...], axis=0) * scale2).T
    mixed = jnp.zeros((C1, LB), F32)
    for j in range(J):
        for k in range(KZ):
            q = j * KZ + k
            p = J * KZ + q
            re = st[q:q + 1]
            im = st[p:p + 1]
            wr = w2[j, 0, k]
            wi = w2[j, 1, k]
            real = jnp.sum(re * wr - im * wi, axis=1, keepdims=True)
            imag = jnp.sum(re * wi + im * wr, axis=1, keepdims=True)
            mixed = jnp.where(lane == q, real, jnp.where(lane == p, imag, mixed))
    mt2[...] = mixed
    ag2[b] = mixed
    gather(mt2, ag2, 2)
    loads[6].wait()
    expand(mt2, ag2, yi2, yb2, ya2, 2, 2)
    for i in range(KX):
        for ch in range(2):
            part = slice(ch * LB, (ch + 1) * LB)
            yr2[i, :, part] = rot_i(ya2[i // IL, i % IL, :, part])

    FC = cells_x * KX

    def fine_step(group, carry):
        parts = []
        for xx in range(GROUP):
            x = group * GROUP + xx
            acc = jnp.zeros((C1, 2 * LB), F32)
            for i in range(KX):
                c = cs_ref[a, 2 * HC + x * KX + i]
                s = cs_ref[a, 2 * HC + FC + x * KX + i]
                acc = acc + (c * ya2[i // IL, i % IL] + s * yr2[i])
            parts.append(acc)
        near = jnp.concatenate([fk_ref[group * GROUP + xx] for xx in range(GROUP)], axis=0)
        for ch in range(2):
            lines = jnp.concatenate([part[:, ch * LB:(ch + 1) * LB] for part in parts], axis=0)
            v = mul(tall(split(lines)), tzi_ref[...])
            rows = []
            for xx in range(0, GROUP, 2):
                half = nar.at[group * (GROUP // 2) + xx // 2]
                pieces = []
                for yy in range(YB):
                    at = (ch * YB + yy) // 2 * zn
                    pieces.append(half[:, at:at + zn])
                rows += [jnp.concatenate(pieces, axis=1) + bo_col] * 2
            g = split(gelu(v + jnp.concatenate(rows, axis=0)))
            cols = slice(ch * width, (ch + 1) * width)
            res = mul(pr_bd, deep(g)) + mul(pl_bd, near[:, cols])
            for xx in range(GROUP):
                o_ref[group * GROUP + xx, :, cols] = res[xx * CIN:(xx + 1) * CIN]
        return carry

    lax.fori_loop(0, cells_x // GROUP, fine_step, 0)
    for copy in sends:
        copy.wait_send()


def on_device(
    A, B, fields, lift, lift_bias, spectral_in, bypass_in, bias_in, spectral_out, bypass_out,
    bias_out, proj, proj_bias,
):
    cin, xc, yc, zc = fields.shape
    C1 = lift.shape[0]
    C2 = bypass_in.shape[0]
    NX = xc * A
    NY = yc * B
    IL = KX // A
    H = B // IL
    J = KY // H
    N = A * B
    width = YB * zc
    cells = float(NX * NY * zc)
    back = math.sqrt(2.0 / (KX * KY * KZ))

    tz = z_table(zc)
    tzf = stacked(tz)
    tzi = stacked(np.ascontiguousarray(tz.T) * back)
    fine_x = x_angles(A, xc, NX)
    half_x = x_angles(A, xc // 2, NX // 2)
    eye = np.eye(cin)
    tx = np.stack([
        np.concatenate([np.kron(np.cos(fine_x[i].T), eye), np.kron(np.sin(fine_x[i].T), eye)], axis=1)
        for i in range(A)
    ])
    cs = np.concatenate([
        np.cos(half_x).reshape(A, -1), np.sin(half_x).reshape(A, -1),
        np.cos(fine_x).reshape(A, -1), np.sin(fine_x).reshape(A, -1),
    ], axis=1).astype(np.float32)
    yf1 = y_table(B, yc, NY, H)
    yfc = y_table(B, yc // 2, NY // 2, H)

    def per_device(table):
        return jnp.asarray(np.ascontiguousarray(np.swapaxes(halves(table), 0, 1)))

    tx_t = per_device(tx)
    yf1_t = per_device(yf1)
    yfc_t = per_device(yfc)
    yic_t = per_device(np.swapaxes(yfc, 1, 2))
    yi2_t = per_device(np.swapaxes(yf1, 1, 2))

    rows = jnp.transpose(fields, (1, 0, 2, 3)).reshape(xc * cin, yc * zc)
    weights2 = jnp.swapaxes(spectral_out, 3, 4)

    vmem = pl.BlockSpec(memory_space=pltpu.VMEM)
    anywhere = pl.BlockSpec(memory_space=pl.ANY)
    V = pltpu.VMEM
    out = pl.pallas_call(
        functools.partial(
            kernel, A, B, xc, 1.0 / math.sqrt(cells), 1.0 / math.sqrt(cells / 4.0), math.sqrt(cells)
        ),
        out_shape=jax.ShapeDtypeStruct((xc, cin, yc * zc), F32),
        in_specs=[vmem] * 10 + [pl.BlockSpec(memory_space=pltpu.SMEM)] + [anywhere] * 8,
        out_specs=vmem,
        scratch_shapes=[
            V(tzi.shape, BF16), V(spectral_in.shape, F32), V(weights2.shape, F32),
            V(tx_t.shape[1:], BF16), V(yf1_t.shape[1:], BF16), V(yfc_t.shape[1:], BF16),
            V(yic_t.shape[1:], BF16), V(yi2_t.shape[1:], BF16),
            V((N, cin, LB), F32), V((N, cin, LB), F32), V((LB, LB), F32),
            V((C2, LB), F32), V((B, C2, LB), F32),
            V((IL, C2, LB), F32), V((A, IL, C2, LB), F32),
            V((xc // 2, C2, LB), F32), V((A, IL, C2, LB), F32), V((A, IL, C2, LB), F32),
            V((B, C2, LB), F32), V((B, C2, LB), F32),
            V((C1, LB), F32), V((B, C1, LB), F32),
            V((IL, C1, 2 * LB), F32), V((A, IL, C1, 2 * LB), F32),
            V((xc // 2, C1, width), F32), V((KX, C2, LB), F32), V((KX, C1, 2 * LB), F32),
            V((xc // 2, 16, width), BF16), V((xc, 16, yc * zc), BF16), V((16, yc * zc), F32), V((GROUP * C2, GROUP * C2), F32),
            pltpu.SemaphoreType.DMA((8,)),
            pltpu.SemaphoreType.DMA((N + 3 * B + 3 * KX,)), pltpu.SemaphoreType.DMA((N + 3 * B + 3 * KX,)),
        ],
        compiler_params=pltpu.CompilerParams(
            collective_id=0, has_side_effects=True, vmem_limit_bytes=60 * 1024 * 1024
        ),
    )(
        rows, lift.T, lift_bias[None], bypass_in.T, bias_in[None], bypass_out, bias_out[None], proj,
        proj_bias[None], jnp.asarray(tzf), jnp.asarray(cs),
        jnp.asarray(tzi), spectral_in, weights2, tx_t, yf1_t, yfc_t, yic_t, yi2_t,
    )
    return jnp.transpose(out.reshape(xc, cin, yc, zc), (1, 0, 2, 3))


def solution(mesh):
    A = mesh.shape["gx"]
    B = mesh.shape["gy"]
    in_specs = (
        P(None, "gx", "gy", None), P(), P(), P(("gx", "gy"), None, None, None, None), P(), P(),
        P(("gx", "gy"), None, None, None, None), P(), P(), P(), P(),
    )
    return jax.shard_map(
        functools.partial(on_device, A, B), mesh=mesh, in_specs=in_specs,
        out_specs=P(None, "gx", "gy", None), check_vma=False,
    )
```
